32 devices in a mesh: grp: 2 (over y), ctx: 4 (over z), head: 2 (over x), sub: 2 (over core).
Axes of the slice: x: 2, y: 2, z: 4, core: 2. Of those that a mesh axis runs over, the one named last changes fastest.
Arguments:
- queries: bfloat16 [512, 16384], P(('grp', 'ctx', 'head', 'sub')), parts along dimension 0, may hold values from -400 to 400
- kv_cache: bfloat16 [2, 8192, 1024], P(None, ('grp', 'ctx', 'sub'), 'head'), parts along dimension 1, may hold values from -6 to 6
- page_counts: int32 [8], P('grp'), parts along dimension 0, may hold values from 1 to 4, as said below
Outputs:
- attended: bfloat16 [512, 16384], P(('grp', 'ctx', 'head', 'sub')), parts along dimension 0
The draws below stay inside these ranges and needn't reach their ends.
There are 2 independent parts, one for each index of `grp`. The reference program is written for one: setup_inputs(seed, part) draws one part's arguments, and reference() takes and returns one part's arrays. A program takes and returns all parts, laid end to end along the dimension named above; each array names one. Nothing has to cross between parts.
Inputs may be any that keep to these rules, and one draw needn't show every extreme that they name: `page_counts`: each count is at least 1, the counts sum to exactly 8, and one request has exactly 4 pages.
All inputs are finite; a program needn't handle non-finite values.
Results may differ from the reference program's by a relative error of at most 0.014.
Values may be sent and summed in bfloat16 or wider, within the bound.
A program may use at most 64 MiB of HBM per device.

```python
import jax
import jax.numpy as jnp
from jax import lax

HQ = 128
KVH = 8
HD = 128
REQS = 4
QR = 64
PAGE = 256
SPAN = 256
CTX = 4096
LIVE_PAGES = 8


def page_split(key):
    largest = LIVE_PAGES // 2
    first_key, second_key, shuffle_key = jax.random.split(jax.random.fold_in(key, 11), 3)
    first_cut = jax.random.randint(first_key, (), 1, largest - 1)
    second_cut = jax.random.randint(second_key, (), 1, largest - first_cut)
    counts = jnp.stack([jnp.int32(largest), first_cut, second_cut, largest - first_cut - second_cut]).astype(jnp.int32)
    shuffle = jax.random.permutation(shuffle_key, REQS)
    return counts[shuffle]


def cache_field(key):
    field_values = jax.random.normal(jax.random.fold_in(key, 23), (2, CTX, KVH * HD), jnp.float32)
    field_values = jnp.clip(field_values, -6.0, 6.0)
    return field_values


def draw_page_counts(key, part):
    return page_split(key)


def draw_kv_cache(key, part):
    return cache_field(key).astype(jnp.bfloat16)


def draw_queries(key, part):
    drawn = jax.random.normal(jax.random.fold_in(key, 37), (SPAN, HQ * HD), jnp.float32)
    field_values = 2.5 * jnp.clip(drawn, -6.0, 6.0)
    return field_values.astype(jnp.bfloat16)


def setup_inputs(seed: int = 0, part: int = 0) -> dict:
    streams_of = jax.random.split(jax.random.key(seed), 4)
    own_keys = jax.random.split(jax.random.fold_in(streams_of[3], part), 4)
    return {
        "queries": draw_queries(jax.random.fold_in(jax.random.fold_in(streams_of[3], part), 71), part),
        "kv_cache": draw_kv_cache(jax.random.fold_in(jax.random.fold_in(streams_of[3], part), 71), part),
        "page_counts": draw_page_counts(jax.random.fold_in(jax.random.fold_in(streams_of[3], part), 71), part),
    }


NEG = -1e30


def reference(queries, kv_cache, page_counts):
    per_group = HQ // KVH
    live = LIVE_PAGES * PAGE
    base = CTX - live
    page_ends = jnp.cumsum(page_counts).astype(jnp.int32) * PAGE
    page_starts = page_ends - page_counts.astype(jnp.int32) * PAGE
    cache_keys = kv_cache[0, base:].astype(jnp.float32).reshape(live, KVH, HD)
    cache_values = kv_cache[1, base:].astype(jnp.float32).reshape(live, KVH, HD)
    grouped = queries.astype(jnp.float32).reshape(REQS, QR, KVH, per_group, HD)
    places = jnp.arange(live, dtype=jnp.int32)
    offsets = jnp.arange(QR, dtype=jnp.int32)
    score_scale = HD ** -0.5

    def one_request(request):
        query_pos = page_ends[request] - QR + offsets
        visible = (places[None, :] >= page_starts[request]) & (places[None, :] <= query_pos[:, None])
        request_rows = grouped[request]

        def one_head(head_id):
            query_head = request_rows[:, head_id]
            key_head = cache_keys[:, head_id]
            value_head = cache_values[:, head_id]
            scores = jnp.einsum('qgd,pd->qgp', query_head, key_head) * score_scale
            scores = jnp.where(visible[:, None, :], scores, NEG)
            top_score = jnp.max(scores, axis=2, keepdims=True)
            numerators = jnp.exp(scores - top_score)
            totals = jnp.sum(numerators, axis=2)
            weights = numerators.astype(jnp.bfloat16).astype(jnp.float32)
            return jnp.einsum('qgp,pd->qgd', weights, value_head) / totals[..., None]

        heads_out = lax.map(one_head, jnp.arange(KVH, dtype=jnp.int32))
        return jnp.transpose(heads_out, (1, 0, 2, 3))

    result = lax.map(one_request, jnp.arange(REQS, dtype=jnp.int32))
    return result.reshape(SPAN, HQ * HD).astype(jnp.bfloat16)
```

```python
import functools
import math

import jax
import jax.numpy as jnp
from jax import lax
from jax.experimental import pallas as pl
from jax.experimental.pallas import tpu as pltpu
from jax.sharding import PartitionSpec as P

HQ = 128
KVH = 8
HD = 128
REQS = 4
QR = 64
PAGE = 256
SPAN = 256


NEG = -1e30
MESH = pl.DeviceIdType.MESH
ROW_BLOCK = 256


def from_behind(array, axis, by):
    count = lax.axis_size(axis)
    pairs = [(i, i + by) for i in range(count) if 0 <= i + by < count]
    return lax.ppermute(array, axis, pairs)


def per_device(queries, kv_cache, page_counts):
    per_group = HQ // KVH
    local_heads = kv_cache.shape[2] // HD
    ctx_size = lax.axis_size("ctx")
    sub_size = lax.axis_size("sub")
    head_count = lax.axis_size("head")
    tok_rows = queries.shape[0]
    score_scale = HD ** (-0.5)
    regrouped = lax.all_to_all(queries, "head", split_axis=1, concat_axis=0, tiled=True)
    all_queries = lax.all_gather(regrouped, ("ctx", "sub"), axis=0, tiled=True)
    all_queries = all_queries.reshape(SPAN, local_heads, per_group, HD)
    page_ends = jnp.cumsum(page_counts)
    ctx_rows = SPAN // ctx_size
    offsets = jnp.arange(QR, dtype=jnp.int32)
    columns = jnp.arange(PAGE, dtype=jnp.int32)
    flat_index = lax.axis_index("ctx") * sub_size + lax.axis_index("sub")
    pages_here = kv_cache.shape[1] // PAGE
    base_pages = pages_here * ctx_size * sub_size // 2
    initial = (
        jnp.full((SPAN, local_heads, per_group), NEG, jnp.float32),
        jnp.zeros((SPAN, local_heads, per_group), jnp.float32),
        jnp.zeros((SPAN, local_heads, per_group, HD), jnp.float32),
    )
    half_rows = kv_cache.shape[1] // 2
    arrived = from_behind(kv_cache[:, half_rows:], "ctx", -(ctx_size // 2))
    is_lower = lax.axis_index("ctx") < ctx_size // 2
    source_flat = flat_index + ctx_size // 2 * sub_size
    working = jnp.where(is_lower, arrived, kv_cache[:, :half_rows])
    first_page = jnp.where(
        is_lower, source_flat * pages_here + pages_here // 2, flat_index * pages_here
    )
    page_total = working.shape[1] // PAGE

    def add_page(page_turn, running):
        page_index = first_page + page_turn
        relative = page_index - base_pages
        counted = jnp.sum((relative >= page_ends).astype(jnp.int32))
        request = jnp.where(relative < 0, REQS, counted)

        def update(partial_value):
            run_max, run_sum, run_out = partial_value
            request_id = jnp.minimum(request, REQS - 1)
            row_start = request_id * QR
            gathered = row_start + offsets
            within = gathered % ctx_rows
            ctx_block = gathered // ctx_rows
            sub_part = within // (head_count * tok_rows)
            head_part = within // tok_rows % head_count
            tok_part = within % tok_rows
            natural = ctx_block * ctx_rows + (head_part * sub_size + sub_part) * tok_rows + tok_part
            query_pos = (page_ends[request_id] + base_pages) * PAGE - QR + natural - row_start
            key_pos = page_index * PAGE + columns
            visible = key_pos[None, :] <= query_pos[:, None]
            page_keys = working[0].reshape(PAGE, local_heads, HD)
            page_values = working[1].reshape(PAGE, local_heads, HD)
            query_rows = lax.dynamic_slice_in_dim(all_queries, row_start, QR, 0)
            scores = (
                jnp.einsum(
                    "qkgd,pkd->qkgp", query_rows, page_keys, preferred_element_type=jnp.float32
                )
                * score_scale
            )
            scores = jnp.where(visible[:, None, None, :], scores, NEG)
            old_max = lax.dynamic_slice_in_dim(run_max, row_start, QR, 0)
            old_sum = lax.dynamic_slice_in_dim(run_sum, row_start, QR, 0)
            old_out = lax.dynamic_slice_in_dim(run_out, row_start, QR, 0)
            new_max = jnp.maximum(old_max, jnp.max(scores, axis=3))
            factor = jnp.exp(old_max - new_max)
            numerators = jnp.exp(scores - new_max[..., None])
            new_sum = old_sum * factor + jnp.sum(numerators, axis=3)
            product = jnp.einsum(
                "qkgp,pkd->qkgd",
                numerators.astype(jnp.bfloat16),
                page_values,
                preferred_element_type=jnp.float32,
            )
            new_out = old_out * factor[..., None] + product
            return (
                lax.dynamic_update_slice_in_dim(run_max, new_max, row_start, 0),
                lax.dynamic_update_slice_in_dim(run_sum, new_sum, row_start, 0),
                lax.dynamic_update_slice_in_dim(run_out, new_out, row_start, 0),
            )

        def unchanged(partial_value):
            return partial_value

        return lax.cond(request < REQS, update, unchanged, running)

    run_max, run_sum, run_out = lax.fori_loop(0, page_total, add_page, initial)
    share = SPAN // (ctx_size * sub_size)
    global_max = lax.pmax(run_max, ("ctx", "sub"))
    factor = jnp.exp(run_max - global_max)
    sums_here, outs_here = (
        lax.psum_scatter(
            (run_sum * factor).astype(jnp.bfloat16), ("ctx", "sub"), scatter_dimension=0, tiled=True
        ).astype(jnp.float32),
        lax.psum_scatter(
            (run_out * factor[..., None]).astype(jnp.bfloat16),
            ("ctx", "sub"),
            scatter_dimension=0,
            tiled=True,
        ).astype(jnp.float32),
    )
    finished = (outs_here / sums_here[..., None]).astype(jnp.bfloat16)
    finished = finished.reshape(share, local_heads * per_group * HD)
    return lax.all_to_all(finished, "head", split_axis=0, concat_axis=1, tiled=True)


def page_plan(ctx_size, sub_size, pages_here):
    live = pages_here * ctx_size * sub_size // 2
    base = live
    last = ctx_size - 1
    low = [0 if r == 0 else live // 2 if r == last else r for r in range(ctx_size)]
    high = [live // 2 if r == 0 else live if r == last else live - (last - r) for r in range(ctx_size)]
    plane_of = [(base + p) // (pages_here * sub_size) for p in range(live)]
    core_of = [(base + p) // pages_here % sub_size for p in range(live)]
    return live, low, high, plane_of, core_of


def can_ship(mesh, rows):
    ctx_size, sub_size, head_size = mesh.shape["ctx"], mesh.shape["sub"], mesh.shape["head"]
    if ctx_size != REQS or SPAN // ctx_size != QR:
        return False
    pages_here = rows // (mesh.shape["grp"] * ctx_size * sub_size) // PAGE
    if pages_here < 1 or KVH % (head_size * sub_size):
        return False
    live, low, high, plane_of, _ = page_plan(ctx_size, sub_size, pages_here)
    ahead = any(
        low[r] <= p < high[r] and r > plane_of[p] for r in range(ctx_size) for p in range(live)
    )
    return not ahead


def ship_kernel(
    sizes,
    counts_ref,
    q_hbm,
    kv_hbm,
    out_hbm,
    kvbuf,
    qbuf,
    qs,
    sbuf,
    mx,
    lsum,
    acc,
    obuf,
    q_send,
    q_recv,
    o_send,
    o_recv,
    kv_send,
    kv_recv,
    relay_send,
):
    ctx_size, sub_size, head_size, pages_here, local_heads = sizes
    live, low, high, plane_of, core_of = page_plan(ctx_size, sub_size, pages_here)
    per_core = local_heads // sub_size
    group = HQ // KVH
    width = group * HD
    plane_devices = head_size * sub_size
    tok_rows = QR // plane_devices
    z, x, s = lax.axis_index("ctx"), lax.axis_index("head"), lax.axis_index("sub")
    mine = x * sub_size + s
    rows = QR * group

    def pick(values):
        got = jnp.int32(values[0])
        for i in range(1, ctx_size):
            got = jnp.where(z == i, jnp.int32(values[i]), got)
        return got

    def here(r, p):
        return low[r] <= p < high[r]

    barrier = pltpu.get_barrier_semaphore()
    for step in range(1, plane_devices):
        other = lax.rem(mine + step, plane_devices)
        pl.semaphore_signal(
            barrier,
            device_id={"head": other // sub_size, "sub": other % sub_size},
            device_id_type=MESH,
        )
    for core in range(sub_size):
        @pl.when(z > 0)
        def _():
            pl.semaphore_signal(
                barrier, device_id={"ctx": z - 1, "sub": core}, device_id_type=MESH
            )

        @pl.when(z < ctx_size - 1)
        def _():
            pl.semaphore_signal(
                barrier, device_id={"ctx": z + 1, "sub": core}, device_id_type=MESH
            )
    amounts = [
        plane_devices - 1 + (sub_size if r > 0 else 0) + (sub_size if r < ctx_size - 1 else 0)
        for r in range(ctx_size)
    ]
    pl.semaphore_wait(barrier, pick(amounts))

    def q_cols(device, h):
        return pl.ds(pl.multiple_of((device * per_core + h) * width, width), width)

    def q_copy(h, step):
        other = lax.rem(mine + step, plane_devices)
        return pltpu.make_async_remote_copy(
            src_ref=q_hbm.at[:, q_cols(other, h)],
            dst_ref=qbuf.at[h, mine],
            send_sem=q_send.at[h, step],
            recv_sem=q_recv.at[h, mine],
            device_id={"head": other // sub_size, "sub": other % sub_size},
            device_id_type=MESH,
        )

    def q_own(h):
        return pltpu.make_async_copy(
            q_hbm.at[:, q_cols(mine, h)], qbuf.at[h, mine], q_recv.at[h, mine]
        )

    def o_copy(h, step):
        other = lax.rem(mine + step, plane_devices)
        return pltpu.make_async_remote_copy(
            src_ref=obuf.at[h, other],
            dst_ref=out_hbm.at[:, q_cols(mine, h)],
            send_sem=o_send.at[h, step],
            recv_sem=o_recv.at[h, mine],
            device_id={"head": other // sub_size, "sub": other % sub_size},
            device_id_type=MESH,
        )

    def o_own(h):
        return pltpu.make_async_copy(
            obuf.at[h, mine], out_hbm.at[:, q_cols(mine, h)], o_recv.at[h, mine]
        )

    def kv_source(h, k, p, core):
        row = p % pages_here * PAGE
        col = (core * per_core + h) * HD
        return kv_hbm.at[k, pl.ds(row, PAGE), pl.ds(pl.multiple_of(col, HD), HD)]

    def kv_remote(h, k, p, slot, core, target):
        return pltpu.make_async_remote_copy(
            src_ref=kv_source(h, k, p, core),
            dst_ref=kvbuf.at[h, k, p],
            send_sem=kv_send.at[h, k, slot, p],
            recv_sem=kv_recv.at[h, k, p],
            device_id=target,
            device_id_type=MESH,
        )

    def kv_own(h, k, p):
        return pltpu.make_async_copy(
            kv_source(h, k, p, s), kvbuf.at[h, k, p], kv_recv.at[h, k, p]
        )

    def each_source(h, k, remote_act, own_act):
        for p in range(live):
            @pl.when((z == plane_of[p]) & (s == core_of[p]))
            def _():
                if plane_of[p] > 0 and any(here(r, p) for r in range(plane_of[p])):
                    for core in range(sub_size):
                        remote_act(
                            kv_remote(h, k, p, core, core, {"ctx": z - 1, "sub": core})
                        )
                if here(plane_of[p], p):
                    for step in range(1, sub_size):
                        other = lax.rem(s + step, sub_size)
                        remote_act(
                            kv_remote(h, k, p, sub_size - 1 + step, other, {"sub": other})
                        )
                    if own_act is not None:
                        own_act(kv_own(h, k, p))

    def relay(h, k, p):
        return pltpu.make_async_remote_copy(
            src_ref=kvbuf.at[h, k, p],
            dst_ref=kvbuf.at[h, k, p],
            send_sem=relay_send.at[h, k, p],
            recv_sem=kv_recv.at[h, k, p],
            device_id={"ctx": z - 1},
            device_id_type=MESH,
        )

    takes = [
        [
            p
            for p in range(live)
            if (plane_of[p] > r and any(here(i, p) for i in range(r + 1))) or here(r, p)
        ]
        for r in range(ctx_size)
    ]
    passes = [
        [p for p in range(live) if plane_of[p] > r and any(here(i, p) for i in range(r))]
        for r in range(ctx_size)
    ]
    take_low, take_high = pick([t[0] for t in takes]), pick([t[-1] + 1 for t in takes])
    pass_low = pick([t[0] if t else 0 for t in passes])
    pass_high = pick([t[-1] + 1 if t else 0 for t in passes])
    own_low, own_high = pick(low), pick(high)

    first = jnp.int32(0)
    for r in range(REQS):
        first = first + jnp.where(z > r, counts_ref[r], 0)
    count = jnp.int32(0)
    for r in range(REQS):
        count = count + jnp.where(z == r, counts_ref[r], 0)
    first_pos = first * PAGE
    query_base = (first + count) * PAGE - QR
    token = lax.broadcasted_iota(jnp.int32, (QR, PAGE), 0)
    column = lax.broadcasted_iota(jnp.int32, (QR, PAGE), 1)
    factor = HD ** (-0.5) * math.log2(math.e)
    block = ROW_BLOCK
    heads_in_block = block // QR

    def start(copy):
        copy.start()

    order = [(h, k) for h in range(per_core) for k in range(2)]
    each_source(0, 0, start, start)
    for h in range(per_core):
        for step in range(1, plane_devices):
            q_copy(h, step).start()
        q_own(h).start()

    for turn, (h, k) in enumerate(order):
        if k == 0:
            for device in range(plane_devices):
                pltpu.make_async_copy(
                    q_hbm.at[:, q_cols(0, h)], qbuf.at[h, device], q_recv.at[h, device]
                ).wait()
            for j in range(group):
                for device in range(plane_devices):
                    qs[pl.ds(j * QR + device * tok_rows, tok_rows), :] = qbuf[
                        h, device, :, j * HD : (j + 1) * HD
                    ]
            mx[...] = jnp.full_like(mx, NEG)
        else:
            for b in range(rows // block):
                sl = pl.ds(b * block, block)
                mx[sl, :] = jnp.broadcast_to(
                    jnp.max(mx[sl, :], axis=1, keepdims=True), (block, HD)
                )
            lsum[...] = jnp.zeros_like(lsum)
            acc[...] = jnp.zeros_like(acc)

        def turn_page(p, carry, h=h, k=k):
            pltpu.make_async_copy(
                kv_source(h, k, 0, 0), kvbuf.at[h, k, p], kv_recv.at[h, k, p]
            ).wait()

            @pl.when((p >= pass_low) & (p < pass_high))
            def _():
                relay(h, k, p).start()

            @pl.when((p >= own_low) & (p < own_high))
            def _():
                field = kvbuf[h, k, p]
                slot = p - own_low
                if k == 0:
                    pos = p * PAGE + column
                    seen = (pos >= first_pos) & (pos <= query_base + token)
                    bias = jnp.where(seen, 0.0, NEG)
                    for b in range(rows // block):
                        sl = pl.ds(b * block, block)
                        scores = lax.dot_general(
                            qs[sl, :],
                            field,
                            (((1,), (1,)), ((), ())),
                            preferred_element_type=jnp.float32,
                        )
                        scores = scores.reshape(heads_in_block, QR, PAGE) + bias[None]
                        scores = scores.reshape(block, PAGE)
                        sbuf[slot, sl, :] = scores
                        top = mx[sl, :]
                        for c in range(PAGE // HD):
                            top = jnp.maximum(top, scores[:, c * HD : (c + 1) * HD])
                        mx[sl, :] = top
                else:
                    for b in range(rows // block):
                        sl = pl.ds(b * block, block)
                        top = mx[sl, :]
                        parts = [
                            jnp.exp2((sbuf[slot, sl, c * HD : (c + 1) * HD] - top) * factor)
                            for c in range(PAGE // HD)
                        ]
                        total = lsum[sl, :]
                        for part in parts:
                            total = total + part
                        lsum[sl, :] = total
                        weights = jnp.concatenate(
                            [part.astype(jnp.bfloat16) for part in parts], axis=1
                        )
                        acc[sl, :] += jnp.dot(
                            weights, field, preferred_element_type=jnp.float32
                        )

            return carry

        lax.fori_loop(take_low, take_high, turn_page, 0)
        if turn + 1 < len(order):
            each_source(*order[turn + 1], start, start)
        if k == 1:
            for j in range(group):
                sl = pl.ds(j * QR, QR)
                done = acc[sl, :] / jnp.sum(lsum[sl, :], axis=1, keepdims=True)
                done = done.astype(jnp.bfloat16)
                for device in range(plane_devices):
                    obuf[h, device, :, j * HD : (j + 1) * HD] = done[
                        device * tok_rows : (device + 1) * tok_rows, :
                    ]
            for step in range(1, plane_devices):
                o_copy(h, step).start()
            o_own(h).start()

    for h in range(per_core):
        for device in range(plane_devices):
            pltpu.make_async_copy(
                obuf.at[h, device], out_hbm.at[:, q_cols(0, h)], o_recv.at[h, device]
            ).wait()
        for step in range(1, plane_devices):
            q_copy(h, step).wait_send()
            o_copy(h, step).wait_send()
        for k in range(2):
            each_source(h, k, lambda copy: copy.wait_send(), None)

            def drain(p, carry, h=h, k=k):
                relay(h, k, p).wait_send()
                return carry

            lax.fori_loop(pass_low, pass_high, drain, 0)


def shipped(queries, kv_cache, page_counts):
    ctx_size, sub_size = lax.axis_size("ctx"), lax.axis_size("sub")
    head_size = lax.axis_size("head")
    local_heads = kv_cache.shape[2] // HD
    pages_here = kv_cache.shape[1] // PAGE
    per_core = local_heads // sub_size
    group = HQ // KVH
    live, low, high, _, _ = page_plan(ctx_size, sub_size, pages_here)
    slots = max(b - a for a, b in zip(low, high))
    plane_devices = head_size * sub_size
    tok_rows = queries.shape[0]
    rows = QR * group
    dma = pltpu.SemaphoreType.DMA
    return pl.pallas_call(
        functools.partial(ship_kernel, (ctx_size, sub_size, head_size, pages_here, local_heads)),
        out_shape=jax.ShapeDtypeStruct(queries.shape, jnp.bfloat16),
        in_specs=[
            pl.BlockSpec(memory_space=pltpu.SMEM),
            pl.BlockSpec(memory_space=pl.ANY),
            pl.BlockSpec(memory_space=pl.ANY),
        ],
        out_specs=pl.BlockSpec(memory_space=pl.ANY),
        scratch_shapes=[
            pltpu.VMEM((per_core, 2, live, PAGE, HD), jnp.bfloat16),
            pltpu.VMEM((per_core, plane_devices, tok_rows, group * HD), jnp.bfloat16),
            pltpu.VMEM((rows, HD), jnp.bfloat16),
            pltpu.VMEM((slots, rows, PAGE), jnp.float32),
            pltpu.VMEM((rows, HD), jnp.float32),
            pltpu.VMEM((rows, HD), jnp.float32),
            pltpu.VMEM((rows, HD), jnp.float32),
            pltpu.VMEM((per_core, plane_devices, tok_rows, group * HD), jnp.bfloat16),
            dma((per_core, plane_devices)),
            dma((per_core, plane_devices)),
            dma((per_core, plane_devices)),
            dma((per_core, plane_devices)),
            dma((per_core, 2, 2 * sub_size - 1, live)),
            dma((per_core, 2, live)),
            dma((per_core, 2, live)),
        ],
        compiler_params=pltpu.CompilerParams(
            collective_id=0, has_side_effects=True, vmem_limit_bytes=40 * 1024 * 1024
        ),
    )(page_counts, queries, kv_cache)


def solution(mesh):
    specs = dict(
        mesh=mesh,
        in_specs=(
            P(("grp", "ctx", "head", "sub"), None),
            P(None, ("grp", "ctx", "sub"), "head"),
            P("grp"),
        ),
        out_specs=P(("grp", "ctx", "head", "sub"), None),
        check_vma=False,
    )

    def run(queries, kv_cache, page_counts):
        body = shipped if can_ship(mesh, kv_cache.shape[1]) else per_device
        return jax.shard_map(body, **specs)(queries, kv_cache, page_counts)

    return run
```

```python
import functools
import math

import jax
import jax.numpy as jnp
from jax import lax
from jax.experimental import pallas as pl
from jax.experimental.pallas import tpu as pltpu
from jax.sharding import PartitionSpec as P

HQ = 128
KVH = 8
HD = 128
REQS = 4
QR = 64
PAGE = 256
SPAN = 256


NEG = -1e30
MESH = pl.DeviceIdType.MESH
ROW_BLOCK = 256


def from_behind(array, axis, by):
    count = lax.axis_size(axis)
    pairs = [(i, i + by) for i in range(count) if 0 <= i + by < count]
    return lax.ppermute(array, axis, pairs)


def per_device(queries, kv_cache, page_counts):
    per_group = HQ // KVH
    local_heads = kv_cache.shape[2] // HD
    ctx_size = lax.axis_size("ctx")
    sub_size = lax.axis_size("sub")
    head_count = lax.axis_size("head")
    tok_rows = queries.shape[0]
    score_scale = HD ** (-0.5)
    regrouped = lax.all_to_all(queries, "head", split_axis=1, concat_axis=0, tiled=True)
    all_queries = lax.all_gather(regrouped, ("ctx", "sub"), axis=0, tiled=True)
    all_queries = all_queries.reshape(SPAN, local_heads, per_group, HD)
    page_ends = jnp.cumsum(page_counts)
    ctx_rows = SPAN // ctx_size
    offsets = jnp.arange(QR, dtype=jnp.int32)
    columns = jnp.arange(PAGE, dtype=jnp.int32)
    flat_index = lax.axis_index("ctx") * sub_size + lax.axis_index("sub")
    pages_here = kv_cache.shape[1] // PAGE
    base_pages = pages_here * ctx_size * sub_size // 2
    initial = (
        jnp.full((SPAN, local_heads, per_group), NEG, jnp.float32),
        jnp.zeros((SPAN, local_heads, per_group), jnp.float32),
        jnp.zeros((SPAN, local_heads, per_group, HD), jnp.float32),
    )
    half_rows = kv_cache.shape[1] // 2
    arrived = from_behind(kv_cache[:, half_rows:], "ctx", -(ctx_size // 2))
    is_lower = lax.axis_index("ctx") < ctx_size // 2
    source_flat = flat_index + ctx_size // 2 * sub_size
    working = jnp.where(is_lower, arrived, kv_cache[:, :half_rows])
    first_page = jnp.where(
        is_lower, source_flat * pages_here + pages_here // 2, flat_index * pages_here
    )
    page_total = working.shape[1] // PAGE

    def add_page(page_turn, running):
        page_index = first_page + page_turn
        relative = page_index - base_pages
        counted = jnp.sum((relative >= page_ends).astype(jnp.int32))
        request = jnp.where(relative < 0, REQS, counted)

        def update(partial_value):
            run_max, run_sum, run_out = partial_value
            request_id = jnp.minimum(request, REQS - 1)
            row_start = request_id * QR
            gathered = row_start + offsets
            within = gathered % ctx_rows
            ctx_block = gathered // ctx_rows
            sub_part = within // (head_count * tok_rows)
            head_part = within // tok_rows % head_count
            tok_part = within % tok_rows
            natural = ctx_block * ctx_rows + (head_part * sub_size + sub_part) * tok_rows + tok_part
            query_pos = (page_ends[request_id] + base_pages) * PAGE - QR + natural - row_start
            key_pos = page_index * PAGE + columns
            visible = key_pos[None, :] <= query_pos[:, None]
            page_keys = working[0].reshape(PAGE, local_heads, HD)
            page_values = working[1].reshape(PAGE, local_heads, HD)
            query_rows = lax.dynamic_slice_in_dim(all_queries, row_start, QR, 0)
            scores = (
                jnp.einsum(
                    "qkgd,pkd->qkgp", query_rows, page_keys, preferred_element_type=jnp.float32
                )
                * score_scale
            )
            scores = jnp.where(visible[:, None, None, :], scores, NEG)
            old_max = lax.dynamic_slice_in_dim(run_max, row_start, QR, 0)
            old_sum = lax.dynamic_slice_in_dim(run_sum, row_start, QR, 0)
            old_out = lax.dynamic_slice_in_dim(run_out, row_start, QR, 0)
            new_max = jnp.maximum(old_max, jnp.max(scores, axis=3))
            factor = jnp.exp(old_max - new_max)
            numerators = jnp.exp(scores - new_max[..., None])
            new_sum = old_sum * factor + jnp.sum(numerators, axis=3)
            product = jnp.einsum(
                "qkgp,pkd->qkgd",
                numerators.astype(jnp.bfloat16),
                page_values,
                preferred_element_type=jnp.float32,
            )
            new_out = old_out * factor[..., None] + product
            return (
                lax.dynamic_update_slice_in_dim(run_max, new_max, row_start, 0),
                lax.dynamic_update_slice_in_dim(run_sum, new_sum, row_start, 0),
                lax.dynamic_update_slice_in_dim(run_out, new_out, row_start, 0),
            )

        def unchanged(partial_value):
            return partial_value

        return lax.cond(request < REQS, update, unchanged, running)

    run_max, run_sum, run_out = lax.fori_loop(0, page_total, add_page, initial)
    share = SPAN // (ctx_size * sub_size)
    global_max = lax.pmax(run_max, ("ctx", "sub"))
    factor = jnp.exp(run_max - global_max)
    sums_here, outs_here = (
        lax.psum_scatter(
            (run_sum * factor).astype(jnp.bfloat16), ("ctx", "sub"), scatter_dimension=0, tiled=True
        ).astype(jnp.float32),
        lax.psum_scatter(
            (run_out * factor[..., None]).astype(jnp.bfloat16),
            ("ctx", "sub"),
            scatter_dimension=0,
            tiled=True,
        ).astype(jnp.float32),
    )
    finished = (outs_here / sums_here[..., None]).astype(jnp.bfloat16)
    finished = finished.reshape(share, local_heads * per_group * HD)
    return lax.all_to_all(finished, "head", split_axis=0, concat_axis=1, tiled=True)


def page_plan(ctx_size, sub_size, pages_here):
    live = pages_here * ctx_size * sub_size // 2
    base = live
    last = ctx_size - 1
    low = [0 if r == 0 else live // 2 if r == last else r for r in range(ctx_size)]
    high = [live // 2 if r == 0 else live if r == last else live - (last - r) for r in range(ctx_size)]
    plane_of = [(base + p) // (pages_here * sub_size) for p in range(live)]
    core_of = [(base + p) // pages_here % sub_size for p in range(live)]
    return live, low, high, plane_of, core_of


def can_ship(mesh, rows):
    ctx_size, sub_size, head_size = mesh.shape["ctx"], mesh.shape["sub"], mesh.shape["head"]
    if ctx_size != REQS or SPAN // ctx_size != QR:
        return False
    pages_here = rows // (mesh.shape["grp"] * ctx_size * sub_size) // PAGE
    if pages_here < 1 or KVH % (head_size * sub_size):
        return False
    live, low, high, plane_of, _ = page_plan(ctx_size, sub_size, pages_here)
    ahead = any(
        low[r] <= p < high[r] and r > plane_of[p] for r in range(ctx_size) for p in range(live)
    )
    return not ahead


def ship_kernel(
    sizes,
    counts_ref,
    q_hbm,
    kv_hbm,
    out_hbm,
    kvbuf,
    qbuf,
    qs,
    sbuf,
    mx,
    lsum,
    acc,
    obuf,
    q_send,
    q_recv,
    o_send,
    o_recv,
    kv_send,
    kv_recv,
    relay_send,
):
    ctx_size, sub_size, head_size, pages_here, local_heads = sizes
    live, low, high, plane_of, core_of = page_plan(ctx_size, sub_size, pages_here)
    hub = plane_of[0]
    per_core = local_heads // sub_size
    moved = per_core - per_core // 2
    group = HQ // KVH
    width = group * HD
    plane_devices = head_size * sub_size
    tok_rows = QR // plane_devices
    z, x, s = lax.axis_index("ctx"), lax.axis_index("head"), lax.axis_index("sub")
    mine = x * sub_size + s
    rows = QR * group

    def pick(values):
        got = jnp.int32(values[0])
        for i in range(1, ctx_size):
            got = jnp.where(z == i, jnp.int32(values[i]), got)
        return got

    def here(r, p):
        return low[r] <= p < high[r]

    def unit_of(h, r):
        return h if h < moved else moved + (h - moved) * (hub + 1) + r

    def whole_plane(a, b):
        return per_core > moved and ((a < hub and b == hub) or (b < hub and a == hub))

    def at(device, plane=None):
        place = {"head": device // sub_size, "sub": device % sub_size}
        if plane is not None:
            place["ctx"] = plane
        return place

    barrier = pltpu.get_barrier_semaphore()
    for step in range(1, plane_devices):
        other = lax.rem(mine + step, plane_devices)
        pl.semaphore_signal(barrier, device_id=at(other), device_id_type=MESH)
    amounts = []
    for a in range(ctx_size):
        amount = plane_devices - 1
        for b in range(ctx_size):
            if a == b or not (whole_plane(a, b) or abs(a - b) == 1):
                continue
            amount += plane_devices if whole_plane(a, b) else sub_size

            @pl.when(z == a)
            def _():
                if whole_plane(a, b):
                    for device in range(plane_devices):
                        pl.semaphore_signal(
                            barrier, device_id=at(device, b), device_id_type=MESH
                        )
                else:
                    for core in range(sub_size):
                        pl.semaphore_signal(
                            barrier, device_id={"ctx": b, "sub": core}, device_id_type=MESH
                        )

        amounts.append(amount)
    pl.semaphore_wait(barrier, pick(amounts))

    def q_cols(device, h):
        return pl.ds(pl.multiple_of((device * per_core + h) * width, width), width)

    def q_copy(h, step):
        other = lax.rem(mine + step, plane_devices)
        return pltpu.make_async_remote_copy(
            src_ref=q_hbm.at[:, q_cols(other, h)],
            dst_ref=qbuf.at[unit_of(h, hub), mine],
            send_sem=q_send.at[h, step],
            recv_sem=q_recv.at[unit_of(h, hub), mine],
            device_id=at(other),
            device_id_type=MESH,
        )

    def q_own(h):
        return pltpu.make_async_copy(
            q_hbm.at[:, q_cols(mine, h)],
            qbuf.at[unit_of(h, hub), mine],
            q_recv.at[unit_of(h, hub), mine],
        )

    def q_up(h, step):
        other = lax.rem(mine + step, plane_devices)
        unit = unit_of(h, lax.rem(z, hub + 1))
        return pltpu.make_async_remote_copy(
            src_ref=q_hbm.at[:, q_cols(other, h)],
            dst_ref=qbuf.at[unit, mine],
            send_sem=q_send.at[h, step],
            recv_sem=q_recv.at[unit, mine],
            device_id=at(other, hub),
            device_id_type=MESH,
        )

    def o_copy(h, step):
        other = lax.rem(mine + step, plane_devices)
        return pltpu.make_async_remote_copy(
            src_ref=obuf.at[unit_of(h, hub), other],
            dst_ref=out_hbm.at[:, q_cols(mine, h)],
            send_sem=o_send.at[unit_of(h, hub), step],
            recv_sem=o_recv.at[h, mine],
            device_id=at(other),
            device_id_type=MESH,
        )

    def o_own(h):
        return pltpu.make_async_copy(
            obuf.at[unit_of(h, hub), mine], out_hbm.at[:, q_cols(mine, h)], o_recv.at[h, mine]
        )

    def o_down(h, r, step):
        other = lax.rem(mine + step, plane_devices)
        return pltpu.make_async_remote_copy(
            src_ref=obuf.at[unit_of(h, r), other],
            dst_ref=out_hbm.at[:, q_cols(mine, h)],
            send_sem=o_send.at[unit_of(h, r), step],
            recv_sem=o_recv.at[h, mine],
            device_id=at(other, r),
            device_id_type=MESH,
        )

    def kv_source(h, k, p, core):
        row = p % pages_here * PAGE
        col = (core * per_core + h) * HD
        return kv_hbm.at[k, pl.ds(row, PAGE), pl.ds(pl.multiple_of(col, HD), HD)]

    def kv_remote(h, k, p, slot, core, target):
        return pltpu.make_async_remote_copy(
            src_ref=kv_source(h, k, p, core),
            dst_ref=kvbuf.at[h, k, p],
            send_sem=kv_send.at[h, k, slot, p],
            recv_sem=kv_recv.at[h, k, p],
            device_id=target,
            device_id_type=MESH,
        )

    def kv_own(h, k, p):
        return pltpu.make_async_copy(
            kv_source(h, k, p, s), kvbuf.at[h, k, p], kv_recv.at[h, k, p]
        )

    def uses(h, r, p):
        if h < moved:
            return here(r, p)
        return r >= hub and any(here(i, p) for i in (range(hub + 1) if r == hub else [r]))

    def hands_down(h, r, p):
        return any(uses(h, i, p) for i in range(r))

    def each_source(h, k, remote_act, own_act):
        for p in range(live):
            @pl.when((z == plane_of[p]) & (s == core_of[p]))
            def _():
                if hands_down(h, plane_of[p], p):
                    for core in range(sub_size):
                        remote_act(
                            kv_remote(h, k, p, core, core, {"ctx": z - 1, "sub": core})
                        )
                if uses(h, plane_of[p], p):
                    for step in range(1, sub_size):
                        other = lax.rem(s + step, sub_size)
                        remote_act(
                            kv_remote(h, k, p, sub_size - 1 + step, other, {"sub": other})
                        )
                    if own_act is not None:
                        own_act(kv_own(h, k, p))

    def relay(h, k, p):
        return pltpu.make_async_remote_copy(
            src_ref=kvbuf.at[h, k, p],
            dst_ref=kvbuf.at[h, k, p],
            send_sem=relay_send.at[h, k, p],
            recv_sem=kv_recv.at[h, k, p],
            device_id={"ctx": z - 1},
            device_id_type=MESH,
        )

    def bounds(pages):
        return (
            pick([t[0] if t else 0 for t in pages]),
            pick([t[-1] + 1 if t else 0 for t in pages]),
        )

    def take_bounds(h):
        return bounds(
            [
                [
                    p
                    for p in range(live)
                    if uses(h, r, p) or (plane_of[p] > r and hands_down(h, r, p))
                ]
                for r in range(ctx_size)
            ]
        )

    def pass_bounds(h):
        return bounds(
            [
                [p for p in range(live) if plane_of[p] > r and hands_down(h, r, p)]
                for r in range(ctx_size)
            ]
        )

    token = lax.broadcasted_iota(jnp.int32, (QR, PAGE), 0)
    column = lax.broadcasted_iota(jnp.int32, (QR, PAGE), 1)
    factor = HD ** (-0.5) * math.log2(math.e)
    block = ROW_BLOCK
    heads_in_block = block // QR

    def span_of(r):
        first, count = jnp.int32(0), jnp.int32(0)
        for i in range(REQS):
            first = first + jnp.where(r > i, counts_ref[i], 0)
            count = count + jnp.where(r == i, counts_ref[i], 0)
        return first * PAGE, (first + count) * PAGE - QR

    def load_queries(h, unit):
        for device in range(plane_devices):
            pltpu.make_async_copy(
                q_hbm.at[:, q_cols(0, h)], qbuf.at[unit, device], q_recv.at[unit, device]
            ).wait()
        for j in range(group):
            for device in range(plane_devices):
                qs[pl.ds(j * QR + device * tok_rows, tok_rows), :] = qbuf[
                    unit, device, :, j * HD : (j + 1) * HD
                ]
        mx[...] = jnp.full_like(mx, NEG)

    def close_maxima():
        for b in range(rows // block):
            sl = pl.ds(b * block, block)
            mx[sl, :] = jnp.broadcast_to(jnp.max(mx[sl, :], axis=1, keepdims=True), (block, HD))
        lsum[...] = jnp.zeros_like(lsum)
        acc[...] = jnp.zeros_like(acc)

    def score_page(h, p, slot, span):
        first_pos, query_base = span
        keys = kvbuf[h, 0, p]
        pos = p * PAGE + column
        seen = (pos >= first_pos) & (pos <= query_base + token)
        bias = jnp.where(seen, 0.0, NEG)
        for b in range(rows // block):
            sl = pl.ds(b * block, block)
            scores = lax.dot_general(
                qs[sl, :], keys, (((1,), (1,)), ((), ())), preferred_element_type=jnp.float32
            )
            scores = scores.reshape(heads_in_block, QR, PAGE) + bias[None]
            scores = scores.reshape(block, PAGE)
            sbuf[slot, sl, :] = scores
            top = mx[sl, :]
            for c in range(PAGE // HD):
                top = jnp.maximum(top, scores[:, c * HD : (c + 1) * HD])
            mx[sl, :] = top

    def value_page(h, p, slot):
        values = kvbuf[h, 1, p]
        for b in range(rows // block):
            sl = pl.ds(b * block, block)
            top = mx[sl, :]
            parts = [
                jnp.exp2((sbuf[slot, sl, c * HD : (c + 1) * HD] - top) * factor)
                for c in range(PAGE // HD)
            ]
            total = lsum[sl, :]
            for part in parts:
                total = total + part
            lsum[sl, :] = total
            weights = jnp.concatenate([part.astype(jnp.bfloat16) for part in parts], axis=1)
            acc[sl, :] += jnp.dot(weights, values, preferred_element_type=jnp.float32)

    def finish(unit):
        for j in range(group):
            sl = pl.ds(j * QR, QR)
            done = acc[sl, :] / jnp.sum(lsum[sl, :], axis=1, keepdims=True)
            done = done.astype(jnp.bfloat16)
            for device in range(plane_devices):
                obuf[unit, device, :, j * HD : (j + 1) * HD] = done[
                    device * tok_rows : (device + 1) * tok_rows, :
                ]

    def await_page(h, k, p):
        pltpu.make_async_copy(
            kv_source(h, k, 0, 0), kvbuf.at[h, k, p], kv_recv.at[h, k, p]
        ).wait()

    def start(copy):
        copy.start()

    def own_queries(h):
        for step in range(1, plane_devices):
            q_copy(h, step).start()
        q_own(h).start()

    def own_outputs(h):
        for step in range(1, plane_devices):
            o_copy(h, step).start()
        o_own(h).start()

    own_span = span_of(z)
    own_low, own_high = pick(low), pick(high)

    def stream(h, k, then=None):
        take_low, take_high = take_bounds(h)
        pass_low, pass_high = pass_bounds(h)

        def turn_page(p, carry):
            await_page(h, k, p)

            @pl.when((p >= pass_low) & (p < pass_high))
            def _():
                relay(h, k, p).start()

            @pl.when((p >= own_low) & (p < own_high))
            def _():
                if k == 0:
                    score_page(h, p, p - own_low, own_span)
                else:
                    value_page(h, p, p - own_low)

            return carry

        lax.fori_loop(take_low, take_high, turn_page, 0)

    def own_head(h, between=None):
        load_queries(h, unit_of(h, hub))
        stream(h, 0)
        if between is not None:
            between()
        close_maxima()
        stream(h, 1)
        finish(unit_of(h, hub))
        own_outputs(h)

    order = [(h, k) for h in range(moved) for k in range(2)]
    rest = [(h, k) for h in range(moved, per_core) for k in range(2)]
    each_source(*order[0], start, start)
    for h in range(moved, per_core):
        @pl.when(z < hub)
        def _():
            for step in range(plane_devices):
                q_up(h, step).start()

    for h in range(moved):
        own_queries(h)
    for h in range(moved, per_core):
        @pl.when(z >= hub)
        def _():
            own_queries(h)

    for h, k in rest:
        if k == 0:
            each_source(h, k, start, start)

    @pl.when(z > hub)
    def _():
        for h, k in order[1:]:
            each_source(h, k, start, start)

    for h, k in rest:
        if k == 1:
            each_source(h, k, start, start)

    def rest_of_order(turn):
        if turn < len(order):

            @pl.when(z <= hub)
            def _():
                each_source(*order[turn], start, start)

    for h in range(moved):
        own_head(h, lambda h=h: rest_of_order(2 * h + 1))
        rest_of_order(2 * h + 2)

    for h in range(moved, per_core):
        @pl.when(z > hub)
        def _():
            own_head(h)

        @pl.when(z == hub)
        def _():
            known = min(p for p in range(live) if uses(h, hub, p))
            for r in range(hub + 1):
                unit = unit_of(h, r)
                span = span_of(r)
                load_queries(h, unit)
                for k in range(2):

                    def arrive(p, carry, k=k):
                        await_page(h, k, p)
                        return carry

                    def turn_page(p, carry, k=k, r=r, span=span):
                        if k == 0:
                            score_page(h, p, p - low[r], span)
                        else:
                            value_page(h, p, p - low[r])
                        return carry

                    lax.fori_loop(known, high[r], arrive, 0)
                    if k == 1:
                        close_maxima()
                    lax.fori_loop(low[r], high[r], turn_page, 0)
                known = high[r]
                finish(unit)
                if r < hub:
                    for step in range(plane_devices):
                        o_down(h, r, step).start()
                else:
                    own_outputs(h)

    for h in range(per_core):
        for device in range(plane_devices):
            pltpu.make_async_copy(
                obuf.at[0, device], out_hbm.at[:, q_cols(0, h)], o_recv.at[h, device]
            ).wait()

        def drain_own():
            for step in range(1, plane_devices):
                q_copy(h, step).wait_send()
                o_copy(h, step).wait_send()

        if h < moved:
            drain_own()
        else:
            pl.when(z >= hub)(drain_own)

            @pl.when(z < hub)
            def _():
                for step in range(plane_devices):
                    q_up(h, step).wait_send()

            @pl.when(z == hub)
            def _():
                for r in range(hub):
                    for step in range(plane_devices):
                        o_down(h, r, step).wait_send()

        for k in range(2):
            each_source(h, k, lambda copy: copy.wait_send(), None)

            def drain(p, carry, h=h, k=k):
                relay(h, k, p).wait_send()
                return carry

            lax.fori_loop(*pass_bounds(h), drain, 0)


def shipped(queries, kv_cache, page_counts):
    ctx_size, sub_size = lax.axis_size("ctx"), lax.axis_size("sub")
    head_size = lax.axis_size("head")
    local_heads = kv_cache.shape[2] // HD
    pages_here = kv_cache.shape[1] // PAGE
    per_core = local_heads // sub_size
    group = HQ // KVH
    live, low, high, plane_of, _ = page_plan(ctx_size, sub_size, pages_here)
    units = per_core - per_core // 2 + per_core // 2 * (plane_of[0] + 1)
    slots = max(b - a for a, b in zip(low, high))
    plane_devices = head_size * sub_size
    tok_rows = queries.shape[0]
    rows = QR * group
    dma = pltpu.SemaphoreType.DMA
    return pl.pallas_call(
        functools.partial(ship_kernel, (ctx_size, sub_size, head_size, pages_here, local_heads)),
        out_shape=jax.ShapeDtypeStruct(queries.shape, jnp.bfloat16),
        in_specs=[
            pl.BlockSpec(memory_space=pltpu.SMEM),
            pl.BlockSpec(memory_space=pl.ANY),
            pl.BlockSpec(memory_space=pl.ANY),
        ],
        out_specs=pl.BlockSpec(memory_space=pl.ANY),
        scratch_shapes=[
            pltpu.VMEM((per_core, 2, live, PAGE, HD), jnp.bfloat16),
            pltpu.VMEM((units, plane_devices, tok_rows, group * HD), jnp.bfloat16),
            pltpu.VMEM((rows, HD), jnp.bfloat16),
            pltpu.VMEM((slots, rows, PAGE), jnp.float32),
            pltpu.VMEM((rows, HD), jnp.float32),
            pltpu.VMEM((rows, HD), jnp.float32),
            pltpu.VMEM((rows, HD), jnp.float32),
            pltpu.VMEM((units, plane_devices, tok_rows, group * HD), jnp.bfloat16),
            dma((per_core, plane_devices)),
            dma((units, plane_devices)),
            dma((units, plane_devices)),
            dma((per_core, plane_devices)),
            dma((per_core, 2, 2 * sub_size - 1, live)),
            dma((per_core, 2, live)),
            dma((per_core, 2, live)),
        ],
        compiler_params=pltpu.CompilerParams(
            collective_id=0, has_side_effects=True, vmem_limit_bytes=67043328
        ),
    )(page_counts, queries, kv_cache)


def solution(mesh):
    specs = dict(
        mesh=mesh,
        in_specs=(
            P(("grp", "ctx", "head", "sub"), None),
            P(None, ("grp", "ctx", "sub"), "head"),
            P("grp"),
        ),
        out_specs=P(("grp", "ctx", "head", "sub"), None),
        check_vma=False,
    )

    def run(queries, kv_cache, page_counts):
        body = shipped if can_ship(mesh, kv_cache.shape[1]) else per_device
        return jax.shard_map(body, **specs)(queries, kv_cache, page_counts)

    return run
```

```python
import functools
import math

import jax
import jax.numpy as jnp
from jax import lax
from jax.experimental import pallas as pl
from jax.experimental.pallas import tpu as pltpu
from jax.sharding import PartitionSpec as P

HQ = 128
KVH = 8
HD = 128
REQS = 4
QR = 64
PAGE = 256
SPAN = 256


NEG = -1e30
MESH = pl.DeviceIdType.MESH
ROW_BLOCK = 256


def from_behind(array, axis, by):
    count = lax.axis_size(axis)
    pairs = [(i, i + by) for i in range(count) if 0 <= i + by < count]
    return lax.ppermute(array, axis, pairs)


def per_device(queries, kv_cache, page_counts):
    per_group = HQ // KVH
    local_heads = kv_cache.shape[2] // HD
    ctx_size = lax.axis_size("ctx")
    sub_size = lax.axis_size("sub")
    head_count = lax.axis_size("head")
    tok_rows = queries.shape[0]
    score_scale = HD ** (-0.5)
    regrouped = lax.all_to_all(queries, "head", split_axis=1, concat_axis=0, tiled=True)
    all_queries = lax.all_gather(regrouped, ("ctx", "sub"), axis=0, tiled=True)
    all_queries = all_queries.reshape(SPAN, local_heads, per_group, HD)
    page_ends = jnp.cumsum(page_counts)
    ctx_rows = SPAN // ctx_size
    offsets = jnp.arange(QR, dtype=jnp.int32)
    columns = jnp.arange(PAGE, dtype=jnp.int32)
    flat_index = lax.axis_index("ctx") * sub_size + lax.axis_index("sub")
    pages_here = kv_cache.shape[1] // PAGE
    base_pages = pages_here * ctx_size * sub_size // 2
    initial = (
        jnp.full((SPAN, local_heads, per_group), NEG, jnp.float32),
        jnp.zeros((SPAN, local_heads, per_group), jnp.float32),
        jnp.zeros((SPAN, local_heads, per_group, HD), jnp.float32),
    )
    half_rows = kv_cache.shape[1] // 2
    arrived = from_behind(kv_cache[:, half_rows:], "ctx", -(ctx_size // 2))
    is_lower = lax.axis_index("ctx") < ctx_size // 2
    source_flat = flat_index + ctx_size // 2 * sub_size
    working = jnp.where(is_lower, arrived, kv_cache[:, :half_rows])
    first_page = jnp.where(
        is_lower, source_flat * pages_here + pages_here // 2, flat_index * pages_here
    )
    page_total = working.shape[1] // PAGE

    def add_page(page_turn, running):
        page_index = first_page + page_turn
        relative = page_index - base_pages
        counted = jnp.sum((relative >= page_ends).astype(jnp.int32))
        request = jnp.where(relative < 0, REQS, counted)

        def update(partial_value):
            run_max, run_sum, run_out = partial_value
            request_id = jnp.minimum(request, REQS - 1)
            row_start = request_id * QR
            gathered = row_start + offsets
            within = gathered % ctx_rows
            ctx_block = gathered // ctx_rows
            sub_part = within // (head_count * tok_rows)
            head_part = within // tok_rows % head_count
            tok_part = within % tok_rows
            natural = ctx_block * ctx_rows + (head_part * sub_size + sub_part) * tok_rows + tok_part
            query_pos = (page_ends[request_id] + base_pages) * PAGE - QR + natural - row_start
            key_pos = page_index * PAGE + columns
            visible = key_pos[None, :] <= query_pos[:, None]
            page_keys = working[0].reshape(PAGE, local_heads, HD)
            page_values = working[1].reshape(PAGE, local_heads, HD)
            query_rows = lax.dynamic_slice_in_dim(all_queries, row_start, QR, 0)
            scores = (
                jnp.einsum(
                    "qkgd,pkd->qkgp", query_rows, page_keys, preferred_element_type=jnp.float32
                )
                * score_scale
            )
            scores = jnp.where(visible[:, None, None, :], scores, NEG)
            old_max = lax.dynamic_slice_in_dim(run_max, row_start, QR, 0)
            old_sum = lax.dynamic_slice_in_dim(run_sum, row_start, QR, 0)
            old_out = lax.dynamic_slice_in_dim(run_out, row_start, QR, 0)
            new_max = jnp.maximum(old_max, jnp.max(scores, axis=3))
            factor = jnp.exp(old_max - new_max)
            numerators = jnp.exp(scores - new_max[..., None])
            new_sum = old_sum * factor + jnp.sum(numerators, axis=3)
            product = jnp.einsum(
                "qkgp,pkd->qkgd",
                numerators.astype(jnp.bfloat16),
                page_values,
                preferred_element_type=jnp.float32,
            )
            new_out = old_out * factor[..., None] + product
            return (
                lax.dynamic_update_slice_in_dim(run_max, new_max, row_start, 0),
                lax.dynamic_update_slice_in_dim(run_sum, new_sum, row_start, 0),
                lax.dynamic_update_slice_in_dim(run_out, new_out, row_start, 0),
            )

        def unchanged(partial_value):
            return partial_value

        return lax.cond(request < REQS, update, unchanged, running)

    run_max, run_sum, run_out = lax.fori_loop(0, page_total, add_page, initial)
    share = SPAN // (ctx_size * sub_size)
    global_max = lax.pmax(run_max, ("ctx", "sub"))
    factor = jnp.exp(run_max - global_max)
    sums_here, outs_here = (
        lax.psum_scatter(
            (run_sum * factor).astype(jnp.bfloat16), ("ctx", "sub"), scatter_dimension=0, tiled=True
        ).astype(jnp.float32),
        lax.psum_scatter(
            (run_out * factor[..., None]).astype(jnp.bfloat16),
            ("ctx", "sub"),
            scatter_dimension=0,
            tiled=True,
        ).astype(jnp.float32),
    )
    finished = (outs_here / sums_here[..., None]).astype(jnp.bfloat16)
    finished = finished.reshape(share, local_heads * per_group * HD)
    return lax.all_to_all(finished, "head", split_axis=0, concat_axis=1, tiled=True)


def page_plan(ctx_size, sub_size, pages_here):
    live = pages_here * ctx_size * sub_size // 2
    base = live
    last = ctx_size - 1
    low = [0 if r == 0 else live // 2 if r == last else r for r in range(ctx_size)]
    high = [live // 2 if r == 0 else live if r == last else live - (last - r) for r in range(ctx_size)]
    plane_of = [(base + p) // (pages_here * sub_size) for p in range(live)]
    core_of = [(base + p) // pages_here % sub_size for p in range(live)]
    return live, low, high, plane_of, core_of


def can_ship(mesh, rows):
    ctx_size, sub_size, head_size = mesh.shape["ctx"], mesh.shape["sub"], mesh.shape["head"]
    if ctx_size != REQS or SPAN // ctx_size != QR:
        return False
    pages_here = rows // (mesh.shape["grp"] * ctx_size * sub_size) // PAGE
    if pages_here < 1 or KVH % (head_size * sub_size):
        return False
    live, low, high, plane_of, _ = page_plan(ctx_size, sub_size, pages_here)
    ahead = any(
        low[r] <= p < high[r] and r > plane_of[p] for r in range(ctx_size) for p in range(live)
    )
    return not ahead


def ship_kernel(
    sizes,
    counts_ref,
    q_hbm,
    kv_hbm,
    out_hbm,
    kvbuf,
    qbuf,
    qs,
    sbuf,
    mx,
    lsum,
    acc,
    obuf,
    q_send,
    q_recv,
    o_send,
    o_recv,
    kv_send,
    kv_recv,
    relay_send,
):
    ctx_size, sub_size, head_size, pages_here, local_heads = sizes
    live, low, high, plane_of, core_of = page_plan(ctx_size, sub_size, pages_here)
    hub = plane_of[0]
    per_core = local_heads // sub_size
    moved = per_core - per_core // 2
    group = HQ // KVH
    width = group * HD
    plane_devices = head_size * sub_size
    tok_rows = QR // plane_devices
    z, x, s = lax.axis_index("ctx"), lax.axis_index("head"), lax.axis_index("sub")
    mine = x * sub_size + s
    rows = QR * group

    def pick(values):
        got = jnp.int32(values[0])
        for i in range(1, ctx_size):
            got = jnp.where(z == i, jnp.int32(values[i]), got)
        return got

    def here(r, p):
        return low[r] <= p < high[r]

    def unit_of(h, r):
        return h if h < moved else moved + (h - moved) * (hub + 1) + r

    def whole_plane(a, b):
        return per_core > moved and ((a < hub and b == hub) or (b < hub and a == hub))

    def at(device, plane=None):
        place = {"head": device // sub_size, "sub": device % sub_size}
        if plane is not None:
            place["ctx"] = plane
        return place

    barrier = pltpu.get_barrier_semaphore()
    for step in range(1, plane_devices):
        other = lax.rem(mine + step, plane_devices)
        pl.semaphore_signal(barrier, device_id=at(other), device_id_type=MESH)
    amounts = []
    for a in range(ctx_size):
        amount = plane_devices - 1
        for b in range(ctx_size):
            if a == b or not (whole_plane(a, b) or abs(a - b) == 1):
                continue
            amount += plane_devices if whole_plane(a, b) else sub_size

            @pl.when(z == a)
            def _():
                if whole_plane(a, b):
                    for device in range(plane_devices):
                        pl.semaphore_signal(
                            barrier, device_id=at(device, b), device_id_type=MESH
                        )
                else:
                    for core in range(sub_size):
                        pl.semaphore_signal(
                            barrier, device_id={"ctx": b, "sub": core}, device_id_type=MESH
                        )

        amounts.append(amount)
    pl.semaphore_wait(barrier, pick(amounts))

    def q_cols(device, h):
        return pl.ds(pl.multiple_of((device * per_core + h) * width, width), width)

    def q_copy(h, step):
        other = lax.rem(mine + step, plane_devices)
        return pltpu.make_async_remote_copy(
            src_ref=q_hbm.at[:, q_cols(other, h)],
            dst_ref=qbuf.at[unit_of(h, hub), mine],
            send_sem=q_send.at[h, step],
            recv_sem=q_recv.at[unit_of(h, hub), mine],
            device_id=at(other),
            device_id_type=MESH,
        )

    def q_own(h):
        return pltpu.make_async_copy(
            q_hbm.at[:, q_cols(mine, h)],
            qbuf.at[unit_of(h, hub), mine],
            q_recv.at[unit_of(h, hub), mine],
        )

    def q_up(h, step):
        other = lax.rem(mine + step, plane_devices)
        unit = unit_of(h, lax.rem(z, hub + 1))
        return pltpu.make_async_remote_copy(
            src_ref=q_hbm.at[:, q_cols(other, h)],
            dst_ref=qbuf.at[unit, mine],
            send_sem=q_send.at[h, step],
            recv_sem=q_recv.at[unit, mine],
            device_id=at(other, hub),
            device_id_type=MESH,
        )

    def o_copy(h, step):
        other = lax.rem(mine + step, plane_devices)
        return pltpu.make_async_remote_copy(
            src_ref=obuf.at[unit_of(h, hub), other],
            dst_ref=out_hbm.at[:, q_cols(mine, h)],
            send_sem=o_send.at[unit_of(h, hub), step],
            recv_sem=o_recv.at[h, mine],
            device_id=at(other),
            device_id_type=MESH,
        )

    def o_own(h):
        return pltpu.make_async_copy(
            obuf.at[unit_of(h, hub), mine], out_hbm.at[:, q_cols(mine, h)], o_recv.at[h, mine]
        )

    def o_down(h, r, step):
        other = lax.rem(mine + step, plane_devices)
        return pltpu.make_async_remote_copy(
            src_ref=obuf.at[unit_of(h, r), other],
            dst_ref=out_hbm.at[:, q_cols(mine, h)],
            send_sem=o_send.at[unit_of(h, r), step],
            recv_sem=o_recv.at[h, mine],
            device_id=at(other, r),
            device_id_type=MESH,
        )

    def kv_source(h, k, p, core):
        row = p % pages_here * PAGE
        col = (core * per_core + h) * HD
        return kv_hbm.at[k, pl.ds(row, PAGE), pl.ds(pl.multiple_of(col, HD), HD)]

    def kv_remote(h, k, p, slot, core, target):
        return pltpu.make_async_remote_copy(
            src_ref=kv_source(h, k, p, core),
            dst_ref=kvbuf.at[h, k, p],
            send_sem=kv_send.at[h, k, slot, p],
            recv_sem=kv_recv.at[h, k, p],
            device_id=target,
            device_id_type=MESH,
        )

    def kv_own(h, k, p):
        return pltpu.make_async_copy(
            kv_source(h, k, p, s), kvbuf.at[h, k, p], kv_recv.at[h, k, p]
        )

    def uses(h, r, p):
        if h < moved:
            return here(r, p)
        return r >= hub and any(here(i, p) for i in (range(hub + 1) if r == hub else [r]))

    def hands_down(h, r, p):
        return any(uses(h, i, p) for i in range(r))

    def each_source(h, k, remote_act, own_act):
        for p in range(live):
            @pl.when((z == plane_of[p]) & (s == core_of[p]))
            def _():
                if hands_down(h, plane_of[p], p):
                    for core in range(sub_size):
                        remote_act(
                            kv_remote(h, k, p, core, core, {"ctx": z - 1, "sub": core})
                        )
                if uses(h, plane_of[p], p):
                    for step in range(1, sub_size):
                        other = lax.rem(s + step, sub_size)
                        remote_act(
                            kv_remote(h, k, p, sub_size - 1 + step, other, {"sub": other})
                        )
                    if own_act is not None:
                        own_act(kv_own(h, k, p))

    def relay(h, k, p):
        return pltpu.make_async_remote_copy(
            src_ref=kvbuf.at[h, k, p],
            dst_ref=kvbuf.at[h, k, p],
            send_sem=relay_send.at[h, k, p],
            recv_sem=kv_recv.at[h, k, p],
            device_id={"ctx": z - 1},
            device_id_type=MESH,
        )

    def bounds(pages):
        return (
            pick([t[0] if t else 0 for t in pages]),
            pick([t[-1] + 1 if t else 0 for t in pages]),
        )

    def take_bounds(h):
        return bounds(
            [
                [
                    p
                    for p in range(live)
                    if uses(h, r, p) or (plane_of[p] > r and hands_down(h, r, p))
                ]
                for r in range(ctx_size)
            ]
        )

    def pass_bounds(h):
        return bounds(
            [
                [p for p in range(live) if plane_of[p] > r and hands_down(h, r, p)]
                for r in range(ctx_size)
            ]
        )

    token = lax.broadcasted_iota(jnp.int32, (QR, PAGE), 0)
    column = lax.broadcasted_iota(jnp.int32, (QR, PAGE), 1)
    factor = HD ** (-0.5) * math.log2(math.e)
    block = ROW_BLOCK
    heads_in_block = block // QR

    def span_of(r):
        first, count = jnp.int32(0), jnp.int32(0)
        for i in range(REQS):
            first = first + jnp.where(r > i, counts_ref[i], 0)
            count = count + jnp.where(r == i, counts_ref[i], 0)
        return first * PAGE, (first + count) * PAGE - QR

    def load_queries(h, unit):
        for device in range(plane_devices):
            pltpu.make_async_copy(
                q_hbm.at[:, q_cols(0, h)], qbuf.at[unit, device], q_recv.at[unit, device]
            ).wait()
        for j in range(group):
            for device in range(plane_devices):
                qs[pl.ds(j * QR + device * tok_rows, tok_rows), :] = qbuf[
                    unit, device, :, j * HD : (j + 1) * HD
                ]
        mx[...] = jnp.full_like(mx, NEG)

    def close_maxima():
        for b in range(rows // block):
            sl = pl.ds(b * block, block)
            mx[sl, :] = jnp.broadcast_to(jnp.max(mx[sl, :], axis=1, keepdims=True), (block, HD))
        lsum[...] = jnp.zeros_like(lsum)
        acc[...] = jnp.zeros_like(acc)

    def score_page(h, p, slot, span):
        first_pos, query_base = span
        keys = kvbuf[h, 0, p]
        pos = p * PAGE + column
        seen = (pos >= first_pos) & (pos <= query_base + token)
        bias = jnp.where(seen, 0.0, NEG)
        for b in range(rows // block):
            sl = pl.ds(b * block, block)
            scores = lax.dot_general(
                qs[sl, :], keys, (((1,), (1,)), ((), ())), preferred_element_type=jnp.float32
            )
            scores = scores.reshape(heads_in_block, QR, PAGE) + bias[None]
            scores = scores.reshape(block, PAGE)
            sbuf[slot, sl, :] = scores
            top = mx[sl, :]
            for c in range(PAGE // HD):
                top = jnp.maximum(top, scores[:, c * HD : (c + 1) * HD])
            mx[sl, :] = top

    def value_page(h, p, slot):
        values = kvbuf[h, 1, p]
        for b in range(rows // block):
            sl = pl.ds(b * block, block)
            top = mx[sl, :]
            parts = [
                jnp.exp2((sbuf[slot, sl, c * HD : (c + 1) * HD] - top) * factor)
                for c in range(PAGE // HD)
            ]
            total = lsum[sl, :]
            for part in parts:
                total = total + part
            lsum[sl, :] = total
            weights = jnp.concatenate([part.astype(jnp.bfloat16) for part in parts], axis=1)
            acc[sl, :] += jnp.dot(weights, values, preferred_element_type=jnp.float32)

    def finish(unit):
        for j in range(group):
            sl = pl.ds(j * QR, QR)
            done = acc[sl, :] / jnp.sum(lsum[sl, :], axis=1, keepdims=True)
            done = done.astype(jnp.bfloat16)
            for device in range(plane_devices):
                obuf[unit, device, :, j * HD : (j + 1) * HD] = done[
                    device * tok_rows : (device + 1) * tok_rows, :
                ]

    def await_page(h, k, p):
        pltpu.make_async_copy(
            kv_source(h, k, 0, 0), kvbuf.at[h, k, p], kv_recv.at[h, k, p]
        ).wait()

    def start(copy):
        copy.start()

    def own_queries(h):
        for step in range(1, plane_devices):
            q_copy(h, step).start()
        q_own(h).start()

    def own_outputs(h):
        for step in range(1, plane_devices):
            o_copy(h, step).start()
        o_own(h).start()

    own_span = span_of(z)
    own_low, own_high = pick(low), pick(high)

    def stream(h, k, then=None):
        take_low, take_high = take_bounds(h)
        pass_low, pass_high = pass_bounds(h)

        def turn_page(p, carry):
            await_page(h, k, p)

            @pl.when((p >= pass_low) & (p < pass_high))
            def _():
                relay(h, k, p).start()

            @pl.when((p >= own_low) & (p < own_high))
            def _():
                if k == 0:
                    score_page(h, p, p - own_low, own_span)
                else:
                    value_page(h, p, p - own_low)

            return carry

        lax.fori_loop(take_low, take_high, turn_page, 0)

    def own_head(h, between=None):
        load_queries(h, unit_of(h, hub))
        stream(h, 0)
        if between is not None:
            between()
        close_maxima()
        stream(h, 1)
        finish(unit_of(h, hub))
        own_outputs(h)

    order = [(h, k) for h in range(moved) for k in range(2)]
    rest = [(h, k) for h in range(moved, per_core) for k in range(2)]
    each_source(*order[0], start, start)
    for h in range(moved, per_core):
        @pl.when(z < hub)
        def _():
            for step in range(plane_devices):
                q_up(h, step).start()

    for h in range(moved):
        own_queries(h)
    for h in range(moved, per_core):
        @pl.when(z >= hub)
        def _():
            own_queries(h)

    @pl.when(z > hub)
    def _():
        for h, k in order[1:]:
            each_source(h, k, start, start)

    for h, k in rest:
        each_source(h, k, start, start)

    def rest_of_order(turn):
        if turn < len(order):

            @pl.when(z <= hub)
            def _():
                each_source(*order[turn], start, start)

    for h in range(moved):
        own_head(h, lambda h=h: rest_of_order(2 * h + 1))
        rest_of_order(2 * h + 2)

    for h in range(moved, per_core):
        @pl.when(z > hub)
        def _():
            own_head(h)

        @pl.when(z == hub)
        def _():
            known = min(p for p in range(live) if uses(h, hub, p))
            for r in range(hub + 1):
                unit = unit_of(h, r)
                span = span_of(r)
                load_queries(h, unit)
                for k in range(2):

                    def arrive(p, carry, k=k):
                        await_page(h, k, p)
                        return carry

                    def turn_page(p, carry, k=k, r=r, span=span):
                        if k == 0:
                            score_page(h, p, p - low[r], span)
                        else:
                            value_page(h, p, p - low[r])
                        return carry

                    lax.fori_loop(known, high[r], arrive, 0)
                    if k == 1:
                        close_maxima()
                    lax.fori_loop(low[r], high[r], turn_page, 0)
                known = high[r]
                finish(unit)
                if r < hub:
                    for step in range(plane_devices):
                        o_down(h, r, step).start()
                else:
                    own_outputs(h)

    for h in range(per_core):
        for device in range(plane_devices):
            pltpu.make_async_copy(
                obuf.at[0, device], out_hbm.at[:, q_cols(0, h)], o_recv.at[h, device]
            ).wait()

        def drain_own():
            for step in range(1, plane_devices):
                q_copy(h, step).wait_send()
                o_copy(h, step).wait_send()

        if h < moved:
            drain_own()
        else:
            pl.when(z >= hub)(drain_own)

            @pl.when(z < hub)
            def _():
                for step in range(plane_devices):
                    q_up(h, step).wait_send()

            @pl.when(z == hub)
            def _():
                for r in range(hub):
                    for step in range(plane_devices):
                        o_down(h, r, step).wait_send()

        for k in range(2):
            each_source(h, k, lambda copy: copy.wait_send(), None)

            def drain(p, carry, h=h, k=k):
                relay(h, k, p).wait_send()
                return carry

            lax.fori_loop(*pass_bounds(h), drain, 0)


def shipped(queries, kv_cache, page_counts):
    ctx_size, sub_size = lax.axis_size("ctx"), lax.axis_size("sub")
    head_size = lax.axis_size("head")
    local_heads = kv_cache.shape[2] // HD
    pages_here = kv_cache.shape[1] // PAGE
    per_core = local_heads // sub_size
    group = HQ // KVH
    live, low, high, plane_of, _ = page_plan(ctx_size, sub_size, pages_here)
    units = per_core - per_core // 2 + per_core // 2 * (plane_of[0] + 1)
    slots = max(b - a for a, b in zip(low, high))
    plane_devices = head_size * sub_size
    tok_rows = queries.shape[0]
    rows = QR * group
    dma = pltpu.SemaphoreType.DMA
    return pl.pallas_call(
        functools.partial(ship_kernel, (ctx_size, sub_size, head_size, pages_here, local_heads)),
        out_shape=jax.ShapeDtypeStruct(queries.shape, jnp.bfloat16),
        in_specs=[
            pl.BlockSpec(memory_space=pltpu.SMEM),
            pl.BlockSpec(memory_space=pl.ANY),
            pl.BlockSpec(memory_space=pl.ANY),
        ],
        out_specs=pl.BlockSpec(memory_space=pl.ANY),
        scratch_shapes=[
            pltpu.VMEM((per_core, 2, live, PAGE, HD), jnp.bfloat16),
            pltpu.VMEM((units, plane_devices, tok_rows, group * HD), jnp.bfloat16),
            pltpu.VMEM((rows, HD), jnp.bfloat16),
            pltpu.VMEM((slots, rows, PAGE), jnp.float32),
            pltpu.VMEM((rows, HD), jnp.float32),
            pltpu.VMEM((rows, HD), jnp.float32),
            pltpu.VMEM((rows, HD), jnp.float32),
            pltpu.VMEM((units, plane_devices, tok_rows, group * HD), jnp.bfloat16),
            dma((per_core, plane_devices)),
            dma((units, plane_devices)),
            dma((units, plane_devices)),
            dma((per_core, plane_devices)),
            dma((per_core, 2, 2 * sub_size - 1, live)),
            dma((per_core, 2, live)),
            dma((per_core, 2, live)),
        ],
        compiler_params=pltpu.CompilerParams(
            collective_id=0, has_side_effects=True, vmem_limit_bytes=67043328
        ),
    )(page_counts, queries, kv_cache)


def solution(mesh):
    specs = dict(
        mesh=mesh,
        in_specs=(
            P(("grp", "ctx", "head", "sub"), None),
            P(None, ("grp", "ctx", "sub"), "head"),
            P("grp"),
        ),
        out_specs=P(("grp", "ctx", "head", "sub"), None),
        check_vma=False,
    )

    def run(queries, kv_cache, page_counts):
        body = shipped if can_ship(mesh, kv_cache.shape[1]) else per_device
        return jax.shard_map(body, **specs)(queries, kv_cache, page_counts)

    return run
```

```python
import functools
import math

import jax
import jax.numpy as jnp
from jax import lax
from jax.experimental import pallas as pl
from jax.experimental.pallas import tpu as pltpu
from jax.sharding import PartitionSpec as P

HQ = 128
KVH = 8
HD = 128
REQS = 4
QR = 64
PAGE = 256
SPAN = 256


NEG = -1e30
MESH = pl.DeviceIdType.MESH
ROW_BLOCK = 256


def from_behind(array, axis, by):
    count = lax.axis_size(axis)
    pairs = [(i, i + by) for i in range(count) if 0 <= i + by < count]
    return lax.ppermute(array, axis, pairs)


def per_device(queries, kv_cache, page_counts):
    per_group = HQ // KVH
    local_heads = kv_cache.shape[2] // HD
    ctx_size = lax.axis_size("ctx")
    sub_size = lax.axis_size("sub")
    head_count = lax.axis_size("head")
    tok_rows = queries.shape[0]
    score_scale = HD ** (-0.5)
    regrouped = lax.all_to_all(queries, "head", split_axis=1, concat_axis=0, tiled=True)
    all_queries = lax.all_gather(regrouped, ("ctx", "sub"), axis=0, tiled=True)
    all_queries = all_queries.reshape(SPAN, local_heads, per_group, HD)
    page_ends = jnp.cumsum(page_counts)
    ctx_rows = SPAN // ctx_size
    offsets = jnp.arange(QR, dtype=jnp.int32)
    columns = jnp.arange(PAGE, dtype=jnp.int32)
    flat_index = lax.axis_index("ctx") * sub_size + lax.axis_index("sub")
    pages_here = kv_cache.shape[1] // PAGE
    base_pages = pages_here * ctx_size * sub_size // 2
    initial = (
        jnp.full((SPAN, local_heads, per_group), NEG, jnp.float32),
        jnp.zeros((SPAN, local_heads, per_group), jnp.float32),
        jnp.zeros((SPAN, local_heads, per_group, HD), jnp.float32),
    )
    half_rows = kv_cache.shape[1] // 2
    arrived = from_behind(kv_cache[:, half_rows:], "ctx", -(ctx_size // 2))
    is_lower = lax.axis_index("ctx") < ctx_size // 2
    source_flat = flat_index + ctx_size // 2 * sub_size
    working = jnp.where(is_lower, arrived, kv_cache[:, :half_rows])
    first_page = jnp.where(
        is_lower, source_flat * pages_here + pages_here // 2, flat_index * pages_here
    )
    page_total = working.shape[1] // PAGE

    def add_page(page_turn, running):
        page_index = first_page + page_turn
        relative = page_index - base_pages
        counted = jnp.sum((relative >= page_ends).astype(jnp.int32))
        request = jnp.where(relative < 0, REQS, counted)

        def update(partial_value):
            run_max, run_sum, run_out = partial_value
            request_id = jnp.minimum(request, REQS - 1)
            row_start = request_id * QR
            gathered = row_start + offsets
            within = gathered % ctx_rows
            ctx_block = gathered // ctx_rows
            sub_part = within // (head_count * tok_rows)
            head_part = within // tok_rows % head_count
            tok_part = within % tok_rows
            natural = ctx_block * ctx_rows + (head_part * sub_size + sub_part) * tok_rows + tok_part
            query_pos = (page_ends[request_id] + base_pages) * PAGE - QR + natural - row_start
            key_pos = page_index * PAGE + columns
            visible = key_pos[None, :] <= query_pos[:, None]
            page_keys = working[0].reshape(PAGE, local_heads, HD)
            page_values = working[1].reshape(PAGE, local_heads, HD)
            query_rows = lax.dynamic_slice_in_dim(all_queries, row_start, QR, 0)
            scores = (
                jnp.einsum(
                    "qkgd,pkd->qkgp", query_rows, page_keys, preferred_element_type=jnp.float32
                )
                * score_scale
            )
            scores = jnp.where(visible[:, None, None, :], scores, NEG)
            old_max = lax.dynamic_slice_in_dim(run_max, row_start, QR, 0)
            old_sum = lax.dynamic_slice_in_dim(run_sum, row_start, QR, 0)
            old_out = lax.dynamic_slice_in_dim(run_out, row_start, QR, 0)
            new_max = jnp.maximum(old_max, jnp.max(scores, axis=3))
            factor = jnp.exp(old_max - new_max)
            numerators = jnp.exp(scores - new_max[..., None])
            new_sum = old_sum * factor + jnp.sum(numerators, axis=3)
            product = jnp.einsum(
                "qkgp,pkd->qkgd",
                numerators.astype(jnp.bfloat16),
                page_values,
                preferred_element_type=jnp.float32,
            )
            new_out = old_out * factor[..., None] + product
            return (
                lax.dynamic_update_slice_in_dim(run_max, new_max, row_start, 0),
                lax.dynamic_update_slice_in_dim(run_sum, new_sum, row_start, 0),
                lax.dynamic_update_slice_in_dim(run_out, new_out, row_start, 0),
            )

        def unchanged(partial_value):
            return partial_value

        return lax.cond(request < REQS, update, unchanged, running)

    run_max, run_sum, run_out = lax.fori_loop(0, page_total, add_page, initial)
    share = SPAN // (ctx_size * sub_size)
    global_max = lax.pmax(run_max, ("ctx", "sub"))
    factor = jnp.exp(run_max - global_max)
    sums_here, outs_here = (
        lax.psum_scatter(
            (run_sum * factor).astype(jnp.bfloat16), ("ctx", "sub"), scatter_dimension=0, tiled=True
        ).astype(jnp.float32),
        lax.psum_scatter(
            (run_out * factor[..., None]).astype(jnp.bfloat16),
            ("ctx", "sub"),
            scatter_dimension=0,
            tiled=True,
        ).astype(jnp.float32),
    )
    finished = (outs_here / sums_here[..., None]).astype(jnp.bfloat16)
    finished = finished.reshape(share, local_heads * per_group * HD)
    return lax.all_to_all(finished, "head", split_axis=0, concat_axis=1, tiled=True)


def page_plan(ctx_size, sub_size, pages_here):
    live = pages_here * ctx_size * sub_size // 2
    base = live
    last = ctx_size - 1
    low = [0 if r == 0 else live // 2 if r == last else r for r in range(ctx_size)]
    high = [live // 2 if r == 0 else live if r == last else live - (last - r) for r in range(ctx_size)]
    plane_of = [(base + p) // (pages_here * sub_size) for p in range(live)]
    core_of = [(base + p) // pages_here % sub_size for p in range(live)]
    return live, low, high, plane_of, core_of


def can_ship(mesh, rows):
    ctx_size, sub_size, head_size = mesh.shape["ctx"], mesh.shape["sub"], mesh.shape["head"]
    if ctx_size != REQS or SPAN // ctx_size != QR:
        return False
    pages_here = rows // (mesh.shape["grp"] * ctx_size * sub_size) // PAGE
    if pages_here < 1 or KVH % (head_size * sub_size):
        return False
    live, low, high, plane_of, _ = page_plan(ctx_size, sub_size, pages_here)
    ahead = any(
        low[r] <= p < high[r] and r > plane_of[p] for r in range(ctx_size) for p in range(live)
    )
    return not ahead


def ship_kernel(
    sizes,
    counts_ref,
    q_hbm,
    kv_hbm,
    out_hbm,
    kvbuf,
    qbuf,
    qs,
    sbuf,
    mx,
    lsum,
    acc,
    obuf,
    q_send,
    q_recv,
    o_send,
    o_recv,
    kv_send,
    kv_recv,
    relay_send,
):
    ctx_size, sub_size, head_size, pages_here, local_heads = sizes
    live, low, high, plane_of, core_of = page_plan(ctx_size, sub_size, pages_here)
    hub = plane_of[0]
    per_core = local_heads // sub_size
    moved = per_core - per_core // 2
    group = HQ // KVH
    width = group * HD
    plane_devices = head_size * sub_size
    tok_rows = QR // plane_devices
    z, x, s = lax.axis_index("ctx"), lax.axis_index("head"), lax.axis_index("sub")
    mine = x * sub_size + s
    rows = QR * group

    def pick(values):
        got = jnp.int32(values[0])
        for i in range(1, ctx_size):
            got = jnp.where(z == i, jnp.int32(values[i]), got)
        return got

    def here(r, p):
        return low[r] <= p < high[r]

    def unit_of(h, r):
        return h if h < moved else moved + (h - moved) * (hub + 1) + r

    def whole_plane(a, b):
        return per_core > moved and ((a < hub and b == hub) or (b < hub and a == hub))

    def at(device, plane=None):
        place = {"head": device // sub_size, "sub": device % sub_size}
        if plane is not None:
            place["ctx"] = plane
        return place

    barrier = pltpu.get_barrier_semaphore()
    for step in range(1, plane_devices):
        other = lax.rem(mine + step, plane_devices)
        pl.semaphore_signal(barrier, device_id=at(other), device_id_type=MESH)
    amounts = []
    for a in range(ctx_size):
        amount = plane_devices - 1
        for b in range(ctx_size):
            if a == b or not (whole_plane(a, b) or abs(a - b) == 1):
                continue
            amount += plane_devices if whole_plane(a, b) else sub_size

            @pl.when(z == a)
            def _():
                if whole_plane(a, b):
                    for device in range(plane_devices):
                        pl.semaphore_signal(
                            barrier, device_id=at(device, b), device_id_type=MESH
                        )
                else:
                    for core in range(sub_size):
                        pl.semaphore_signal(
                            barrier, device_id={"ctx": b, "sub": core}, device_id_type=MESH
                        )

        amounts.append(amount)
    pl.semaphore_wait(barrier, pick(amounts))

    def q_cols(device, h):
        return pl.ds(pl.multiple_of((device * per_core + h) * width, width), width)

    def q_copy(h, step):
        other = lax.rem(mine + step, plane_devices)
        return pltpu.make_async_remote_copy(
            src_ref=q_hbm.at[:, q_cols(other, h)],
            dst_ref=qbuf.at[unit_of(h, hub), mine],
            send_sem=q_send.at[h, step],
            recv_sem=q_recv.at[unit_of(h, hub), mine],
            device_id=at(other),
            device_id_type=MESH,
        )

    def q_own(h):
        return pltpu.make_async_copy(
            q_hbm.at[:, q_cols(mine, h)],
            qbuf.at[unit_of(h, hub), mine],
            q_recv.at[unit_of(h, hub), mine],
        )

    def q_up(h, step):
        other = lax.rem(mine + step, plane_devices)
        unit = unit_of(h, lax.rem(z, hub + 1))
        return pltpu.make_async_remote_copy(
            src_ref=q_hbm.at[:, q_cols(other, h)],
            dst_ref=qbuf.at[unit, mine],
            send_sem=q_send.at[h, step],
            recv_sem=q_recv.at[unit, mine],
            device_id=at(other, hub),
            device_id_type=MESH,
        )

    def o_copy(h, step):
        other = lax.rem(mine + step, plane_devices)
        return pltpu.make_async_remote_copy(
            src_ref=obuf.at[unit_of(h, hub), other],
            dst_ref=out_hbm.at[:, q_cols(mine, h)],
            send_sem=o_send.at[unit_of(h, hub), step],
            recv_sem=o_recv.at[h, mine],
            device_id=at(other),
            device_id_type=MESH,
        )

    def o_own(h):
        return pltpu.make_async_copy(
            obuf.at[unit_of(h, hub), mine], out_hbm.at[:, q_cols(mine, h)], o_recv.at[h, mine]
        )

    def o_down(h, r, step):
        other = lax.rem(mine + step, plane_devices)
        return pltpu.make_async_remote_copy(
            src_ref=obuf.at[unit_of(h, r), other],
            dst_ref=out_hbm.at[:, q_cols(mine, h)],
            send_sem=o_send.at[unit_of(h, r), step],
            recv_sem=o_recv.at[h, mine],
            device_id=at(other, r),
            device_id_type=MESH,
        )

    def kv_source(h, k, p, core):
        row = p % pages_here * PAGE
        col = (core * per_core + h) * HD
        return kv_hbm.at[k, pl.ds(row, PAGE), pl.ds(pl.multiple_of(col, HD), HD)]

    def kv_remote(h, k, p, slot, core, target):
        return pltpu.make_async_remote_copy(
            src_ref=kv_source(h, k, p, core),
            dst_ref=kvbuf.at[h, k, p],
            send_sem=kv_send.at[h, k, slot, p],
            recv_sem=kv_recv.at[h, k, p],
            device_id=target,
            device_id_type=MESH,
        )

    def kv_own(h, k, p):
        return pltpu.make_async_copy(
            kv_source(h, k, p, s), kvbuf.at[h, k, p], kv_recv.at[h, k, p]
        )

    def uses(h, r, p):
        if h < moved:
            return here(r, p)
        return r >= hub and any(here(i, p) for i in (range(hub + 1) if r == hub else [r]))

    def hands_down(h, r, p):
        return any(uses(h, i, p) for i in range(r))

    def each_source(h, k, remote_act, own_act):
        for p in range(live):
            @pl.when((z == plane_of[p]) & (s == core_of[p]))
            def _():
                if hands_down(h, plane_of[p], p):
                    for core in range(sub_size):
                        remote_act(
                            kv_remote(h, k, p, core, core, {"ctx": z - 1, "sub": core})
                        )
                if uses(h, plane_of[p], p):
                    for step in range(1, sub_size):
                        other = lax.rem(s + step, sub_size)
                        remote_act(
                            kv_remote(h, k, p, sub_size - 1 + step, other, {"sub": other})
                        )
                    if own_act is not None:
                        own_act(kv_own(h, k, p))

    def relay(h, k, p):
        return pltpu.make_async_remote_copy(
            src_ref=kvbuf.at[h, k, p],
            dst_ref=kvbuf.at[h, k, p],
            send_sem=relay_send.at[h, k, p],
            recv_sem=kv_recv.at[h, k, p],
            device_id={"ctx": z - 1},
            device_id_type=MESH,
        )

    def bounds(pages):
        return (
            pick([t[0] if t else 0 for t in pages]),
            pick([t[-1] + 1 if t else 0 for t in pages]),
        )

    def take_bounds(h):
        return bounds(
            [
                [
                    p
                    for p in range(live)
                    if uses(h, r, p) or (plane_of[p] > r and hands_down(h, r, p))
                ]
                for r in range(ctx_size)
            ]
        )

    def pass_bounds(h):
        return bounds(
            [
                [p for p in range(live) if plane_of[p] > r and hands_down(h, r, p)]
                for r in range(ctx_size)
            ]
        )

    token = lax.broadcasted_iota(jnp.int32, (QR, PAGE), 0)
    column = lax.broadcasted_iota(jnp.int32, (QR, PAGE), 1)
    factor = HD ** (-0.5) * math.log2(math.e)
    block = ROW_BLOCK
    heads_in_block = block // QR

    def span_of(r):
        first, count = jnp.int32(0), jnp.int32(0)
        for i in range(REQS):
            first = first + jnp.where(r > i, counts_ref[i], 0)
            count = count + jnp.where(r == i, counts_ref[i], 0)
        return first * PAGE, (first + count) * PAGE - QR

    def load_queries(h, unit):
        for device in range(plane_devices):
            pltpu.make_async_copy(
                q_hbm.at[:, q_cols(0, h)], qbuf.at[unit, device], q_recv.at[unit, device]
            ).wait()
        for j in range(group):
            for device in range(plane_devices):
                qs[pl.ds(j * QR + device * tok_rows, tok_rows), :] = qbuf[
                    unit, device, :, j * HD : (j + 1) * HD
                ]
        mx[...] = jnp.full_like(mx, NEG)

    def close_maxima():
        for b in range(rows // block):
            sl = pl.ds(b * block, block)
            mx[sl, :] = jnp.broadcast_to(jnp.max(mx[sl, :], axis=1, keepdims=True), (block, HD))
        lsum[...] = jnp.zeros_like(lsum)
        acc[...] = jnp.zeros_like(acc)

    def score_page(h, p, slot, span):
        first_pos, query_base = span
        keys = kvbuf[h, 0, p]
        pos = p * PAGE + column
        seen = (pos >= first_pos) & (pos <= query_base + token)
        bias = jnp.where(seen, 0.0, NEG)
        for b in range(rows // block):
            sl = pl.ds(b * block, block)
            scores = lax.dot_general(
                qs[sl, :], keys, (((1,), (1,)), ((), ())), preferred_element_type=jnp.float32
            )
            scores = scores.reshape(heads_in_block, QR, PAGE) + bias[None]
            scores = scores.reshape(block, PAGE)
            sbuf[slot, sl, :] = scores
            top = mx[sl, :]
            for c in range(PAGE // HD):
                top = jnp.maximum(top, scores[:, c * HD : (c + 1) * HD])
            mx[sl, :] = top

    def value_page(h, p, slot):
        values = kvbuf[h, 1, p]
        for b in range(rows // block):
            sl = pl.ds(b * block, block)
            top = mx[sl, :]
            parts = [
                jnp.exp2((sbuf[slot, sl, c * HD : (c + 1) * HD] - top) * factor)
                for c in range(PAGE // HD)
            ]
            total = lsum[sl, :]
            for part in parts:
                total = total + part
            lsum[sl, :] = total
            weights = jnp.concatenate([part.astype(jnp.bfloat16) for part in parts], axis=1)
            acc[sl, :] += jnp.dot(weights, values, preferred_element_type=jnp.float32)

    def finish(unit):
        for j in range(group):
            sl = pl.ds(j * QR, QR)
            done = acc[sl, :] / jnp.sum(lsum[sl, :], axis=1, keepdims=True)
            done = done.astype(jnp.bfloat16)
            for device in range(plane_devices):
                obuf[unit, device, :, j * HD : (j + 1) * HD] = done[
                    device * tok_rows : (device + 1) * tok_rows, :
                ]

    def await_page(h, k, p):
        pltpu.make_async_copy(
            kv_source(h, k, 0, 0), kvbuf.at[h, k, p], kv_recv.at[h, k, p]
        ).wait()

    def start(copy):
        copy.start()

    def own_queries(h):
        for step in range(1, plane_devices):
            q_copy(h, step).start()
        q_own(h).start()

    def own_outputs(h):
        for step in range(1, plane_devices):
            o_copy(h, step).start()
        o_own(h).start()

    def drain_pages(h):
        for k in range(2):
            each_source(h, k, lambda copy: copy.wait_send(), None)

            def drain(p, carry, k=k):
                relay(h, k, p).wait_send()
                return carry

            lax.fori_loop(*pass_bounds(h), drain, 0)

    own_span = span_of(z)
    own_low, own_high = pick(low), pick(high)

    def stream(h, k, then=None):
        take_low, take_high = take_bounds(h)
        pass_low, pass_high = pass_bounds(h)

        def turn_page(p, carry):
            await_page(h, k, p)

            @pl.when((p >= pass_low) & (p < pass_high))
            def _():
                relay(h, k, p).start()

            @pl.when((p >= own_low) & (p < own_high))
            def _():
                if k == 0:
                    score_page(h, p, p - own_low, own_span)
                else:
                    value_page(h, p, p - own_low)

            return carry

        lax.fori_loop(take_low, take_high, turn_page, 0)

    def own_head(h, between=None):
        load_queries(h, unit_of(h, hub))
        stream(h, 0)
        if between is not None:
            between()
        close_maxima()
        stream(h, 1)
        finish(unit_of(h, hub))
        own_outputs(h)

    order = [(h, k) for h in range(moved) for k in range(2)]
    rest = [(h, k) for h in range(moved, per_core) for k in range(2)]
    each_source(*order[0], start, start)
    for h in range(moved, per_core):
        @pl.when(z < hub)
        def _():
            for step in range(plane_devices):
                q_up(h, step).start()

    for h in range(moved):
        own_queries(h)
    for h in range(moved, per_core):
        @pl.when(z >= hub)
        def _():
            own_queries(h)

    @pl.when(z > hub)
    def _():
        for h, k in order[1:]:
            each_source(h, k, start, start)

    for h, k in rest:
        each_source(h, k, start, start)

    def rest_of_order(turn):
        if turn < len(order):

            @pl.when(z <= hub)
            def _():
                each_source(*order[turn], start, start)

    for h in range(moved):
        own_head(h, lambda h=h: rest_of_order(2 * h + 1))
        rest_of_order(2 * h + 2)

    for h in range(moved, per_core):
        @pl.when(z > hub)
        def _():
            own_head(h)

        @pl.when(z == hub)
        def _():
            known = min(p for p in range(live) if uses(h, hub, p))
            for r in range(hub + 1):
                unit = unit_of(h, r)
                span = span_of(r)
                load_queries(h, unit)
                for k in range(2):

                    def arrive(p, carry, k=k):
                        await_page(h, k, p)
                        return carry

                    def turn_page(p, carry, k=k, r=r, span=span):
                        if k == 0:
                            score_page(h, p, p - low[r], span)
                        else:
                            value_page(h, p, p - low[r])
                        return carry

                    lax.fori_loop(known, high[r], arrive, 0)
                    if k == 1:
                        close_maxima()
                    lax.fori_loop(low[r], high[r], turn_page, 0)
                known = high[r]
                finish(unit)
                if r < hub:
                    if r == 0 and h == moved:
                        for i in range(moved):
                            drain_pages(i)
                    for step in range(plane_devices):
                        o_down(h, r, step).start()
                else:
                    own_outputs(h)

    for h in range(per_core):
        for device in range(plane_devices):
            pltpu.make_async_copy(
                obuf.at[0, device], out_hbm.at[:, q_cols(0, h)], o_recv.at[h, device]
            ).wait()

        def drain_own():
            for step in range(1, plane_devices):
                q_copy(h, step).wait_send()
                o_copy(h, step).wait_send()

        if h < moved:
            drain_own()
        else:
            pl.when(z >= hub)(drain_own)

            @pl.when(z < hub)
            def _():
                for step in range(plane_devices):
                    q_up(h, step).wait_send()

            @pl.when(z == hub)
            def _():
                for r in range(hub):
                    for step in range(plane_devices):
                        o_down(h, r, step).wait_send()

        if h < moved and moved < per_core:

            @pl.when(z != hub)
            def _():
                drain_pages(h)

        else:
            drain_pages(h)


def shipped(queries, kv_cache, page_counts):
    ctx_size, sub_size = lax.axis_size("ctx"), lax.axis_size("sub")
    head_size = lax.axis_size("head")
    local_heads = kv_cache.shape[2] // HD
    pages_here = kv_cache.shape[1] // PAGE
    per_core = local_heads // sub_size
    group = HQ // KVH
    live, low, high, plane_of, _ = page_plan(ctx_size, sub_size, pages_here)
    units = per_core - per_core // 2 + per_core // 2 * (plane_of[0] + 1)
    slots = max(b - a for a, b in zip(low, high))
    plane_devices = head_size * sub_size
    tok_rows = queries.shape[0]
    rows = QR * group
    dma = pltpu.SemaphoreType.DMA
    return pl.pallas_call(
        functools.partial(ship_kernel, (ctx_size, sub_size, head_size, pages_here, local_heads)),
        out_shape=jax.ShapeDtypeStruct(queries.shape, jnp.bfloat16),
        in_specs=[
            pl.BlockSpec(memory_space=pltpu.SMEM),
            pl.BlockSpec(memory_space=pl.ANY),
            pl.BlockSpec(memory_space=pl.ANY),
        ],
        out_specs=pl.BlockSpec(memory_space=pl.ANY),
        scratch_shapes=[
            pltpu.VMEM((per_core, 2, live, PAGE, HD), jnp.bfloat16),
            pltpu.VMEM((units, plane_devices, tok_rows, group * HD), jnp.bfloat16),
            pltpu.VMEM((rows, HD), jnp.bfloat16),
            pltpu.VMEM((slots, rows, PAGE), jnp.float32),
            pltpu.VMEM((rows, HD), jnp.float32),
            pltpu.VMEM((rows, HD), jnp.float32),
            pltpu.VMEM((rows, HD), jnp.float32),
            pltpu.VMEM((units, plane_devices, tok_rows, group * HD), jnp.bfloat16),
            dma((per_core, plane_devices)),
            dma((units, plane_devices)),
            dma((units, plane_devices)),
            dma((per_core, plane_devices)),
            dma((per_core, 2, 2 * sub_size - 1, live)),
            dma((per_core, 2, live)),
            dma((per_core, 2, live)),
        ],
        compiler_params=pltpu.CompilerParams(
            collective_id=0, has_side_effects=True, vmem_limit_bytes=67043328
        ),
    )(page_counts, queries, kv_cache)


def solution(mesh):
    specs = dict(
        mesh=mesh,
        in_specs=(
            P(("grp", "ctx", "head", "sub"), None),
            P(None, ("grp", "ctx", "sub"), "head"),
            P("grp"),
        ),
        out_specs=P(("grp", "ctx", "head", "sub"), None),
        check_vma=False,
    )

    def run(queries, kv_cache, page_counts):
        body = shipped if can_ship(mesh, kv_cache.shape[1]) else per_device
        return jax.shard_map(body, **specs)(queries, kv_cache, page_counts)

    return run
```

```python
import functools
import math

import jax
import jax.numpy as jnp
from jax import lax
from jax.experimental import pallas as pl
from jax.experimental.pallas import tpu as pltpu
from jax.sharding import PartitionSpec as P

HQ = 128
KVH = 8
HD = 128
REQS = 4
QR = 64
PAGE = 256
SPAN = 256


NEG = -1e30
MESH = pl.DeviceIdType.MESH
ROW_BLOCK = 256


def from_behind(array, axis, by):
    count = lax.axis_size(axis)
    pairs = [(i, i + by) for i in range(count) if 0 <= i + by < count]
    return lax.ppermute(array, axis, pairs)


def per_device(queries, kv_cache, page_counts):
    per_group = HQ // KVH
    local_heads = kv_cache.shape[2] // HD
    ctx_size = lax.axis_size("ctx")
    sub_size = lax.axis_size("sub")
    head_count = lax.axis_size("head")
    tok_rows = queries.shape[0]
    score_scale = HD ** (-0.5)
    regrouped = lax.all_to_all(queries, "head", split_axis=1, concat_axis=0, tiled=True)
    all_queries = lax.all_gather(regrouped, ("ctx", "sub"), axis=0, tiled=True)
    all_queries = all_queries.reshape(SPAN, local_heads, per_group, HD)
    page_ends = jnp.cumsum(page_counts)
    ctx_rows = SPAN // ctx_size
    offsets = jnp.arange(QR, dtype=jnp.int32)
    columns = jnp.arange(PAGE, dtype=jnp.int32)
    flat_index = lax.axis_index("ctx") * sub_size + lax.axis_index("sub")
    pages_here = kv_cache.shape[1] // PAGE
    base_pages = pages_here * ctx_size * sub_size // 2
    initial = (
        jnp.full((SPAN, local_heads, per_group), NEG, jnp.float32),
        jnp.zeros((SPAN, local_heads, per_group), jnp.float32),
        jnp.zeros((SPAN, local_heads, per_group, HD), jnp.float32),
    )
    half_rows = kv_cache.shape[1] // 2
    arrived = from_behind(kv_cache[:, half_rows:], "ctx", -(ctx_size // 2))
    is_lower = lax.axis_index("ctx") < ctx_size // 2
    source_flat = flat_index + ctx_size // 2 * sub_size
    working = jnp.where(is_lower, arrived, kv_cache[:, :half_rows])
    first_page = jnp.where(
        is_lower, source_flat * pages_here + pages_here // 2, flat_index * pages_here
    )
    page_total = working.shape[1] // PAGE

    def add_page(page_turn, running):
        page_index = first_page + page_turn
        relative = page_index - base_pages
        counted = jnp.sum((relative >= page_ends).astype(jnp.int32))
        request = jnp.where(relative < 0, REQS, counted)

        def update(partial_value):
            run_max, run_sum, run_out = partial_value
            request_id = jnp.minimum(request, REQS - 1)
            row_start = request_id * QR
            gathered = row_start + offsets
            within = gathered % ctx_rows
            ctx_block = gathered // ctx_rows
            sub_part = within // (head_count * tok_rows)
            head_part = within // tok_rows % head_count
            tok_part = within % tok_rows
            natural = ctx_block * ctx_rows + (head_part * sub_size + sub_part) * tok_rows + tok_part
            query_pos = (page_ends[request_id] + base_pages) * PAGE - QR + natural - row_start
            key_pos = page_index * PAGE + columns
            visible = key_pos[None, :] <= query_pos[:, None]
            page_keys = working[0].reshape(PAGE, local_heads, HD)
            page_values = working[1].reshape(PAGE, local_heads, HD)
            query_rows = lax.dynamic_slice_in_dim(all_queries, row_start, QR, 0)
            scores = (
                jnp.einsum(
                    "qkgd,pkd->qkgp", query_rows, page_keys, preferred_element_type=jnp.float32
                )
                * score_scale
            )
            scores = jnp.where(visible[:, None, None, :], scores, NEG)
            old_max = lax.dynamic_slice_in_dim(run_max, row_start, QR, 0)
            old_sum = lax.dynamic_slice_in_dim(run_sum, row_start, QR, 0)
            old_out = lax.dynamic_slice_in_dim(run_out, row_start, QR, 0)
            new_max = jnp.maximum(old_max, jnp.max(scores, axis=3))
            factor = jnp.exp(old_max - new_max)
            numerators = jnp.exp(scores - new_max[..., None])
            new_sum = old_sum * factor + jnp.sum(numerators, axis=3)
            product = jnp.einsum(
                "qkgp,pkd->qkgd",
                numerators.astype(jnp.bfloat16),
                page_values,
                preferred_element_type=jnp.float32,
            )
            new_out = old_out * factor[..., None] + product
            return (
                lax.dynamic_update_slice_in_dim(run_max, new_max, row_start, 0),
                lax.dynamic_update_slice_in_dim(run_sum, new_sum, row_start, 0),
                lax.dynamic_update_slice_in_dim(run_out, new_out, row_start, 0),
            )

        def unchanged(partial_value):
            return partial_value

        return lax.cond(request < REQS, update, unchanged, running)

    run_max, run_sum, run_out = lax.fori_loop(0, page_total, add_page, initial)
    share = SPAN // (ctx_size * sub_size)
    global_max = lax.pmax(run_max, ("ctx", "sub"))
    factor = jnp.exp(run_max - global_max)
    sums_here, outs_here = (
        lax.psum_scatter(
            (run_sum * factor).astype(jnp.bfloat16), ("ctx", "sub"), scatter_dimension=0, tiled=True
        ).astype(jnp.float32),
        lax.psum_scatter(
            (run_out * factor[..., None]).astype(jnp.bfloat16),
            ("ctx", "sub"),
            scatter_dimension=0,
            tiled=True,
        ).astype(jnp.float32),
    )
    finished = (outs_here / sums_here[..., None]).astype(jnp.bfloat16)
    finished = finished.reshape(share, local_heads * per_group * HD)
    return lax.all_to_all(finished, "head", split_axis=0, concat_axis=1, tiled=True)


def page_plan(ctx_size, sub_size, pages_here):
    live = pages_here * ctx_size * sub_size // 2
    base = live
    last = ctx_size - 1
    low = [0 if r == 0 else live // 2 if r == last else r for r in range(ctx_size)]
    high = [live // 2 if r == 0 else live if r == last else live - (last - r) for r in range(ctx_size)]
    plane_of = [(base + p) // (pages_here * sub_size) for p in range(live)]
    core_of = [(base + p) // pages_here % sub_size for p in range(live)]
    return live, low, high, plane_of, core_of


def can_ship(mesh, rows):
    ctx_size, sub_size, head_size = mesh.shape["ctx"], mesh.shape["sub"], mesh.shape["head"]
    if ctx_size != REQS or SPAN // ctx_size != QR:
        return False
    pages_here = rows // (mesh.shape["grp"] * ctx_size * sub_size) // PAGE
    if pages_here < 1 or KVH % (head_size * sub_size):
        return False
    live, low, high, plane_of, _ = page_plan(ctx_size, sub_size, pages_here)
    ahead = any(
        low[r] <= p < high[r] and r > plane_of[p] for r in range(ctx_size) for p in range(live)
    )
    return not ahead


def ship_kernel(
    sizes,
    counts_ref,
    q_hbm,
    kv_hbm,
    out_hbm,
    kvbuf,
    qbuf,
    qs,
    sbuf,
    mx,
    lsum,
    acc,
    obuf,
    q_send,
    q_recv,
    o_send,
    o_recv,
    kv_send,
    kv_recv,
    relay_send,
):
    ctx_size, sub_size, head_size, pages_here, local_heads = sizes
    live, low, high, plane_of, core_of = page_plan(ctx_size, sub_size, pages_here)
    hub = plane_of[0]
    per_core = local_heads // sub_size
    moved = per_core - per_core // 2
    group = HQ // KVH
    width = group * HD
    plane_devices = head_size * sub_size
    tok_rows = QR // plane_devices
    z, x, s = lax.axis_index("ctx"), lax.axis_index("head"), lax.axis_index("sub")
    mine = x * sub_size + s
    rows = QR * group

    def pick(values):
        got = jnp.int32(values[0])
        for i in range(1, ctx_size):
            got = jnp.where(z == i, jnp.int32(values[i]), got)
        return got

    def here(r, p):
        return low[r] <= p < high[r]

    def unit_of(h, r):
        return h if h < moved else moved + (h - moved) * (hub + 1) + r

    def whole_plane(a, b):
        return per_core > moved and ((a < hub and b == hub) or (b < hub and a == hub))

    def at(device, plane=None):
        place = {"head": device // sub_size, "sub": device % sub_size}
        if plane is not None:
            place["ctx"] = plane
        return place

    barrier = pltpu.get_barrier_semaphore()
    for step in range(1, plane_devices):
        other = lax.rem(mine + step, plane_devices)
        pl.semaphore_signal(barrier, device_id=at(other), device_id_type=MESH)
    amounts = []
    for a in range(ctx_size):
        amount = plane_devices - 1
        for b in range(ctx_size):
            if a == b or not (whole_plane(a, b) or abs(a - b) == 1):
                continue
            amount += plane_devices if whole_plane(a, b) else sub_size

            @pl.when(z == a)
            def _():
                if whole_plane(a, b):
                    for device in range(plane_devices):
                        pl.semaphore_signal(
                            barrier, device_id=at(device, b), device_id_type=MESH
                        )
                else:
                    for core in range(sub_size):
                        pl.semaphore_signal(
                            barrier, device_id={"ctx": b, "sub": core}, device_id_type=MESH
                        )

        amounts.append(amount)
    pl.semaphore_wait(barrier, pick(amounts))

    def q_cols(device, h):
        return pl.ds(pl.multiple_of((device * per_core + h) * width, width), width)

    def q_copy(h, step):
        other = lax.rem(mine + step, plane_devices)
        return pltpu.make_async_remote_copy(
            src_ref=q_hbm.at[:, q_cols(other, h)],
            dst_ref=qbuf.at[unit_of(h, hub), mine],
            send_sem=q_send.at[h, step],
            recv_sem=q_recv.at[unit_of(h, hub), mine],
            device_id=at(other),
            device_id_type=MESH,
        )

    def q_own(h):
        return pltpu.make_async_copy(
            q_hbm.at[:, q_cols(mine, h)],
            qbuf.at[unit_of(h, hub), mine],
            q_recv.at[unit_of(h, hub), mine],
        )

    def q_up(h, step):
        other = lax.rem(mine + step, plane_devices)
        unit = unit_of(h, lax.rem(z, hub + 1))
        return pltpu.make_async_remote_copy(
            src_ref=q_hbm.at[:, q_cols(other, h)],
            dst_ref=qbuf.at[unit, mine],
            send_sem=q_send.at[h, step],
            recv_sem=q_recv.at[unit, mine],
            device_id=at(other, hub),
            device_id_type=MESH,
        )

    def o_copy(h, step):
        other = lax.rem(mine + step, plane_devices)
        return pltpu.make_async_remote_copy(
            src_ref=obuf.at[unit_of(h, hub), other],
            dst_ref=out_hbm.at[:, q_cols(mine, h)],
            send_sem=o_send.at[unit_of(h, hub), step],
            recv_sem=o_recv.at[h, mine],
            device_id=at(other),
            device_id_type=MESH,
        )

    def o_own(h):
        return pltpu.make_async_copy(
            obuf.at[unit_of(h, hub), mine], out_hbm.at[:, q_cols(mine, h)], o_recv.at[h, mine]
        )

    def o_down(h, r, step):
        other = lax.rem(mine + step, plane_devices)
        return pltpu.make_async_remote_copy(
            src_ref=obuf.at[unit_of(h, r), other],
            dst_ref=out_hbm.at[:, q_cols(mine, h)],
            send_sem=o_send.at[unit_of(h, r), step],
            recv_sem=o_recv.at[h, mine],
            device_id=at(other, r),
            device_id_type=MESH,
        )

    def kv_source(h, k, p, core):
        row = p % pages_here * PAGE
        col = (core * per_core + h) * HD
        return kv_hbm.at[k, pl.ds(row, PAGE), pl.ds(pl.multiple_of(col, HD), HD)]

    def kv_remote(h, k, p, slot, core, target):
        return pltpu.make_async_remote_copy(
            src_ref=kv_source(h, k, p, core),
            dst_ref=kvbuf.at[h, k, p],
            send_sem=kv_send.at[h, k, slot, p],
            recv_sem=kv_recv.at[h, k, p],
            device_id=target,
            device_id_type=MESH,
        )

    def kv_own(h, k, p):
        return pltpu.make_async_copy(
            kv_source(h, k, p, s), kvbuf.at[h, k, p], kv_recv.at[h, k, p]
        )

    def uses(h, r, p):
        if h < moved:
            return here(r, p)
        return r >= hub and any(here(i, p) for i in (range(hub + 1) if r == hub else [r]))

    def hands_down(h, r, p):
        return any(uses(h, i, p) for i in range(r))

    def each_source(h, k, remote_act, own_act):
        for p in range(live):
            @pl.when((z == plane_of[p]) & (s == core_of[p]))
            def _():
                if hands_down(h, plane_of[p], p):
                    for core in range(sub_size):
                        remote_act(
                            kv_remote(h, k, p, core, core, {"ctx": z - 1, "sub": core})
                        )
                if uses(h, plane_of[p], p):
                    for step in range(1, sub_size):
                        other = lax.rem(s + step, sub_size)
                        remote_act(
                            kv_remote(h, k, p, sub_size - 1 + step, other, {"sub": other})
                        )
                    if own_act is not None:
                        own_act(kv_own(h, k, p))

    def relay(h, k, p):
        return pltpu.make_async_remote_copy(
            src_ref=kvbuf.at[h, k, p],
            dst_ref=kvbuf.at[h, k, p],
            send_sem=relay_send.at[h, k, p],
            recv_sem=kv_recv.at[h, k, p],
            device_id={"ctx": z - 1},
            device_id_type=MESH,
        )

    def bounds(pages):
        return (
            pick([t[0] if t else 0 for t in pages]),
            pick([t[-1] + 1 if t else 0 for t in pages]),
        )

    def take_bounds(h):
        return bounds(
            [
                [
                    p
                    for p in range(live)
                    if uses(h, r, p) or (plane_of[p] > r and hands_down(h, r, p))
                ]
                for r in range(ctx_size)
            ]
        )

    def pass_bounds(h):
        return bounds(
            [
                [p for p in range(live) if plane_of[p] > r and hands_down(h, r, p)]
                for r in range(ctx_size)
            ]
        )

    token = lax.broadcasted_iota(jnp.int32, (QR, PAGE), 0)
    column = lax.broadcasted_iota(jnp.int32, (QR, PAGE), 1)
    factor = HD ** (-0.5) * math.log2(math.e)
    block = ROW_BLOCK
    heads_in_block = block // QR

    def span_of(r):
        first, count = jnp.int32(0), jnp.int32(0)
        for i in range(REQS):
            first = first + jnp.where(r > i, counts_ref[i], 0)
            count = count + jnp.where(r == i, counts_ref[i], 0)
        return first * PAGE, (first + count) * PAGE - QR

    def load_queries(h, unit):
        for device in range(plane_devices):
            pltpu.make_async_copy(
                q_hbm.at[:, q_cols(0, h)], qbuf.at[unit, device], q_recv.at[unit, device]
            ).wait()
        for j in range(group):
            for device in range(plane_devices):
                qs[pl.ds(j * QR + device * tok_rows, tok_rows), :] = qbuf[
                    unit, device, :, j * HD : (j + 1) * HD
                ]
        mx[...] = jnp.full_like(mx, NEG)

    def close_maxima():
        for b in range(rows // block):
            sl = pl.ds(b * block, block)
            mx[sl, :] = jnp.broadcast_to(jnp.max(mx[sl, :], axis=1, keepdims=True), (block, HD))
        lsum[...] = jnp.zeros_like(lsum)
        acc[...] = jnp.zeros_like(acc)

    def score_page(h, p, slot, span):
        first_pos, query_base = span
        keys = kvbuf[h, 0, p]
        pos = p * PAGE + column
        seen = (pos >= first_pos) & (pos <= query_base + token)
        bias = jnp.where(seen, 0.0, NEG)
        for b in range(rows // block):
            sl = pl.ds(b * block, block)
            scores = lax.dot_general(
                qs[sl, :], keys, (((1,), (1,)), ((), ())), preferred_element_type=jnp.float32
            )
            scores = scores.reshape(heads_in_block, QR, PAGE) + bias[None]
            scores = scores.reshape(block, PAGE)
            sbuf[slot, sl, :] = scores
            top = mx[sl, :]
            for c in range(PAGE // HD):
                top = jnp.maximum(top, scores[:, c * HD : (c + 1) * HD])
            mx[sl, :] = top

    def value_page(h, p, slot):
        values = kvbuf[h, 1, p]
        for b in range(rows // block):
            sl = pl.ds(b * block, block)
            top = mx[sl, :]
            parts = [
                jnp.exp2((sbuf[slot, sl, c * HD : (c + 1) * HD] - top) * factor)
                for c in range(PAGE // HD)
            ]
            total = lsum[sl, :]
            for part in parts:
                total = total + part
            lsum[sl, :] = total
            weights = jnp.concatenate([part.astype(jnp.bfloat16) for part in parts], axis=1)
            acc[sl, :] += jnp.dot(weights, values, preferred_element_type=jnp.float32)

    def finish(unit):
        for j in range(group):
            sl = pl.ds(j * QR, QR)
            done = acc[sl, :] / jnp.sum(lsum[sl, :], axis=1, keepdims=True)
            done = done.astype(jnp.bfloat16)
            for device in range(plane_devices):
                obuf[unit, device, :, j * HD : (j + 1) * HD] = done[
                    device * tok_rows : (device + 1) * tok_rows, :
                ]

    def await_page(h, k, p):
        pltpu.make_async_copy(
            kv_source(h, k, 0, 0), kvbuf.at[h, k, p], kv_recv.at[h, k, p]
        ).wait()

    def start(copy):
        copy.start()

    def own_queries(h):
        for step in range(1, plane_devices):
            q_copy(h, step).start()
        q_own(h).start()

    def own_outputs(h):
        for step in range(1, plane_devices):
            o_copy(h, step).start()
        o_own(h).start()

    def drain_pages(h):
        for k in range(2):
            each_source(h, k, lambda copy: copy.wait_send(), None)

            def drain(p, carry, k=k):
                relay(h, k, p).wait_send()
                return carry

            lax.fori_loop(*pass_bounds(h), drain, 0)

    own_span = span_of(z)
    own_low, own_high = pick(low), pick(high)

    def stream(h, k, then=None):
        take_low, take_high = take_bounds(h)
        pass_low, pass_high = pass_bounds(h)

        def turn_page(p, carry):
            await_page(h, k, p)

            @pl.when((p >= pass_low) & (p < pass_high))
            def _():
                relay(h, k, p).start()

            @pl.when((p >= own_low) & (p < own_high))
            def _():
                if k == 0:
                    score_page(h, p, p - own_low, own_span)
                else:
                    value_page(h, p, p - own_low)

            return carry

        lax.fori_loop(take_low, take_high, turn_page, 0)

    def own_head(h, between=None):
        load_queries(h, unit_of(h, hub))
        stream(h, 0)
        if between is not None:
            between()
        close_maxima()
        stream(h, 1)
        finish(unit_of(h, hub))
        own_outputs(h)

    order = [(h, k) for h in range(moved) for k in range(2)]
    rest = [(h, k) for h in range(moved, per_core) for k in range(2)]
    each_source(*order[0], start, start)
    for h in range(moved, per_core):
        @pl.when(z < hub)
        def _():
            for step in range(plane_devices):
                q_up(h, step).start()

    for h in range(moved):
        own_queries(h)
    for h in range(moved, per_core):
        @pl.when(z >= hub)
        def _():
            own_queries(h)

    for h, k in order[1:] + rest:
        each_source(h, k, start, start)

    for h in range(moved):
        own_head(h)

    for h in range(moved, per_core):
        @pl.when(z > hub)
        def _():
            own_head(h)

        @pl.when(z == hub)
        def _():
            known = min(p for p in range(live) if uses(h, hub, p))
            for r in range(hub + 1):
                unit = unit_of(h, r)
                span = span_of(r)
                load_queries(h, unit)
                for k in range(2):

                    def arrive(p, carry, k=k):
                        await_page(h, k, p)
                        return carry

                    def turn_page(p, carry, k=k, r=r, span=span):
                        if k == 0:
                            score_page(h, p, p - low[r], span)
                        else:
                            value_page(h, p, p - low[r])
                        return carry

                    lax.fori_loop(known, high[r], arrive, 0)
                    if k == 1:
                        close_maxima()
                    lax.fori_loop(low[r], high[r], turn_page, 0)
                known = high[r]
                finish(unit)
                if r < hub:
                    if r == 0 and h == moved:
                        for i in range(moved):
                            drain_pages(i)
                    for step in range(plane_devices):
                        o_down(h, r, step).start()
                else:
                    own_outputs(h)

    for h in range(per_core):
        for device in range(plane_devices):
            pltpu.make_async_copy(
                obuf.at[0, device], out_hbm.at[:, q_cols(0, h)], o_recv.at[h, device]
            ).wait()

        def drain_own():
            for step in range(1, plane_devices):
                q_copy(h, step).wait_send()
                o_copy(h, step).wait_send()

        if h < moved:
            drain_own()
        else:
            pl.when(z >= hub)(drain_own)

            @pl.when(z < hub)
            def _():
                for step in range(plane_devices):
                    q_up(h, step).wait_send()

            @pl.when(z == hub)
            def _():
                for r in range(hub):
                    for step in range(plane_devices):
                        o_down(h, r, step).wait_send()

        if h < moved and moved < per_core:

            @pl.when(z != hub)
            def _():
                drain_pages(h)

        else:
            drain_pages(h)


def shipped(queries, kv_cache, page_counts):
    ctx_size, sub_size = lax.axis_size("ctx"), lax.axis_size("sub")
    head_size = lax.axis_size("head")
    local_heads = kv_cache.shape[2] // HD
    pages_here = kv_cache.shape[1] // PAGE
    per_core = local_heads // sub_size
    group = HQ // KVH
    live, low, high, plane_of, _ = page_plan(ctx_size, sub_size, pages_here)
    units = per_core - per_core // 2 + per_core // 2 * (plane_of[0] + 1)
    slots = max(b - a for a, b in zip(low, high))
    plane_devices = head_size * sub_size
    tok_rows = queries.shape[0]
    rows = QR * group
    dma = pltpu.SemaphoreType.DMA
    return pl.pallas_call(
        functools.partial(ship_kernel, (ctx_size, sub_size, head_size, pages_here, local_heads)),
        out_shape=jax.ShapeDtypeStruct(queries.shape, jnp.bfloat16),
        in_specs=[
            pl.BlockSpec(memory_space=pltpu.SMEM),
            pl.BlockSpec(memory_space=pl.ANY),
            pl.BlockSpec(memory_space=pl.ANY),
        ],
        out_specs=pl.BlockSpec(memory_space=pl.ANY),
        scratch_shapes=[
            pltpu.VMEM((per_core, 2, live, PAGE, HD), jnp.bfloat16),
            pltpu.VMEM((units, plane_devices, tok_rows, group * HD), jnp.bfloat16),
            pltpu.VMEM((rows, HD), jnp.bfloat16),
            pltpu.VMEM((slots, rows, PAGE), jnp.float32),
            pltpu.VMEM((rows, HD), jnp.float32),
            pltpu.VMEM((rows, HD), jnp.float32),
            pltpu.VMEM((rows, HD), jnp.float32),
            pltpu.VMEM((units, plane_devices, tok_rows, group * HD), jnp.bfloat16),
            dma((per_core, plane_devices)),
            dma((units, plane_devices)),
            dma((units, plane_devices)),
            dma((per_core, plane_devices)),
            dma((per_core, 2, 2 * sub_size - 1, live)),
            dma((per_core, 2, live)),
            dma((per_core, 2, live)),
        ],
        compiler_params=pltpu.CompilerParams(
            collective_id=0, has_side_effects=True, vmem_limit_bytes=67043328
        ),
    )(page_counts, queries, kv_cache)


def solution(mesh):
    specs = dict(
        mesh=mesh,
        in_specs=(
            P(("grp", "ctx", "head", "sub"), None),
            P(None, ("grp", "ctx", "sub"), "head"),
            P("grp"),
        ),
        out_specs=P(("grp", "ctx", "head", "sub"), None),
        check_vma=False,
    )

    def run(queries, kv_cache, page_counts):
        body = shipped if can_ship(mesh, kv_cache.shape[1]) else per_device
        return jax.shard_map(body, **specs)(queries, kv_cache, page_counts)

    return run
```
